32 devices in a mesh: comp: 4 (over y, x), dom: 8 (over z, core).
Axes of the slice: x: 2, y: 2, z: 4, core: 2. Of those that a mesh axis runs over, the one named last changes fastest.
Arguments:
- state: float32 [72, 524288], P(None, ('comp', 'dom')), may hold values from -6 to 6
- forcing: float32 [8, 524288], P(None, ('comp', 'dom')), may hold values from -6 to 6
- vertical: float32 [4, 72, 72], P('comp'), may hold values from -0.75 to 0.75
- inject: float32 [4, 72, 8], P('comp'), may hold values from -2 to 2
- extract: float32 [4, 8, 72], P('comp'), may hold values from -0.75 to 0.75
- diffuse: float32 [524288], P(('comp', 'dom')), may hold values from 0.05 to 0.24
- substeps: int32 [524288], P(('comp', 'dom')), may hold values from 1 to 4, as said below
- landmask: int32 [524288], P(('comp', 'dom')), may hold values 0 or 1
- links: int32 [3, 32, 32, 2], P(None, ('comp', 'dom')), may hold values from -1 to 127, as said below
- remap_weight_matrices: float32 [512, 128, 128], P(('comp', 'dom')), may hold values from -0.5 to 0.5
Outputs:
- state_next: float32 [72, 524288], P(None, ('comp', 'dom'))
- forcing_next: float32 [8, 524288], P(None, ('comp', 'dom'))
The draws below stay inside these ranges and needn't reach their ends.
Inputs may be any that keep to these rules, and one draw needn't show every extreme that they name: substeps holds each column's count of substeps; 4 and 1 occur in every draw. In each [g, h, k] either all three fields are -1 (an empty slot) or links[0] and links[1] are blocks 0 to 127 and links[2] a slot 0 to 15; live slots of a pair come first; live entries join an atmosphere device (index below (3) * 8) with an ocean device only, and every such pair has one or more live slots; a pair has at most 2 live slots, and some pair reaches 2 in every draw.
All inputs are finite; a program needn't handle non-finite values. No bound on the sum of `landmask` on one device may be relied on, other than what follows from the above.
Results may differ from the reference program's by a relative error of at most 0.0003.
Values sent between devices are 32-bit elements; how exact they have to be, the bound alone decides.
A program may use at most 128 MiB of HBM per device.

```python
import math
import jax
import jax.numpy as jnp
from jax import lax

LEV = 72
NF = 8
INTERSECT_WIDTH = 128
NB = 128
SLOTS_PER_TARGET = 2
WEIGHT_SLOTS = 16
SUBS = 4
SECTIONS = 4
CELLS = 524288
N_COMP = 4
N_DOM = 8


def draw_substeps(key, part):
    counts = jax.random.randint(key, (N_COMP * N_DOM * NB * INTERSECT_WIDTH,), 1, SUBS + 1)
    return counts.at[0].set(SUBS).at[1].set(1).astype(jnp.int32)


def draw_links(key, part):
    every_device_list = N_COMP * N_DOM
    atmos_count = (N_COMP - 1) * N_DOM
    random_subkeys = jax.random.split(jax.random.fold_in(key, 11), 5)
    is_atmos = jnp.arange(every_device_list) < atmos_count
    partner = (is_atmos[:, None] != is_atmos[None, :]).astype(jnp.int32)
    fuller = jax.random.randint(random_subkeys[0], (every_device_list, every_device_list), 0, 4)
    live_count = jnp.where(fuller > 0, SLOTS_PER_TARGET, jnp.maximum(SLOTS_PER_TARGET - 1, 1)) * partner
    live_count = live_count.at[0, atmos_count].set(SLOTS_PER_TARGET).at[atmos_count, 0].set(SLOTS_PER_TARGET)
    is_live = jnp.arange(SLOTS_PER_TARGET)[None, None, :] < live_count[:, :, None]
    source_block = jax.random.randint(random_subkeys[2], (every_device_list, every_device_list, SLOTS_PER_TARGET), 0, NB)
    target_block = jax.random.randint(random_subkeys[3], (every_device_list, every_device_list, SLOTS_PER_TARGET), 0, NB)
    matrix_slot_index = jax.random.randint(random_subkeys[4], (every_device_list, every_device_list, SLOTS_PER_TARGET), 0, WEIGHT_SLOTS)
    stacked = jnp.stack([source_block, target_block, matrix_slot_index])
    return jnp.where(is_live[None], stacked, -1).astype(jnp.int32)


def set_ends(array, stream_key, least, largest):
    shape = array.shape
    spot = [jax.random.randint(jax.random.fold_in(stream_key, axis), (), 0, shape[axis]) for axis in range(len(shape))]
    array = array.at[tuple(spot)].set(least)
    longest = shape.index(max(shape))
    spot[longest] = (spot[longest] + 1) % shape[longest]
    return array.at[tuple(spot)].set(largest)


def shard_levels(key, extent, pieces, low, high):
    loudness, own = 1.0, jax.random.fold_in(key, 6)
    for dim, parts in pieces:
        draws = jnp.exp(jax.random.uniform(jax.random.fold_in(own, dim), (parts,), jnp.float32, low / len(pieces), high / len(pieces)))
        loudness = loudness * jnp.repeat(draws, extent[dim] // parts).reshape([-1 if axis == dim else 1 for axis in range(len(extent))])
    return loudness


def normal_values(key, extent, width, bound, cuts=(), kind=jnp.bfloat16):
    entries = jax.random.normal(key, extent, jnp.float32) * width
    if len(cuts) > 0:
        entries = shard_levels(key, extent, cuts, -0.22, 0.18) * entries
    return jnp.clip(entries, min=-bound, max=bound).astype(kind)


def setup_inputs(seed: int = 0) -> dict:
    key_list = jax.random.split(jax.random.key(seed), 11)
    state = normal_values(key_list[0], (LEV, CELLS), 1.0, 6.0, ((1, 32),), jnp.float32)
    forcing = normal_values(key_list[1], (NF, CELLS), 1.0, 6.0, ((1, 32),), jnp.float32)
    vertical = normal_values(key_list[2], (SECTIONS, LEV, LEV), LEV ** -0.5, 0.75, ((0, 4),), jnp.float32)
    inject = normal_values(key_list[3], (SECTIONS, LEV, NF), NF ** -0.5, 2.0, ((0, 4),), jnp.float32)
    extract = normal_values(key_list[4], (SECTIONS, NF, LEV), LEV ** -0.5, 0.75, ((0, 4),), jnp.float32)
    diffuse = jnp.clip(jnp.exp(math.log(0.24) - 1.5686159 * jax.random.uniform(key_list[5], (CELLS,), jnp.float32) ** shard_levels(key_list[5], (CELLS,), ((0, 32),), -0.2, 0.2)), 0.05, 0.24)
    substeps = draw_substeps(jax.random.fold_in(key_list[10], 71), 0)
    landmask = set_ends((jax.random.randint(key_list[7], (CELLS,), 0, 4) < 3).astype(jnp.int32), jax.random.fold_in(key_list[7], 1), 0, 1)
    links = draw_links(jax.random.fold_in(key_list[10], 71), 0)
    remap_weight_matrices = normal_values(key_list[9], (N_COMP * N_DOM * WEIGHT_SLOTS, INTERSECT_WIDTH, INTERSECT_WIDTH), INTERSECT_WIDTH ** -0.5, 0.5, ((0, 32),), jnp.float32)
    return dict(state=state, forcing=forcing, vertical=vertical, inject=inject, extract=extract, diffuse=diffuse, substeps=substeps, landmask=landmask, links=links, remap_weight_matrices=remap_weight_matrices)


DT = 0.25


def reference(state, forcing, vertical, inject, extract, diffuse, substeps, landmask, links, remap_weight_matrices):
    highest = lax.Precision.HIGHEST
    every_device_list = N_COMP * N_DOM
    cycle_len = N_DOM * NB * INTERSECT_WIDTH
    wet_cells = landmask.astype(jnp.float32).reshape(1, N_COMP, cycle_len)
    field = state.reshape(LEV, N_COMP, cycle_len)
    coupled = jnp.einsum("sfl,lsc->fsc", extract, field, precision=highest) * wet_cells
    blocks = coupled.reshape(NF, every_device_list, NB, INTERSECT_WIDTH).transpose(1, 2, 0, 3)
    weight_entries = remap_weight_matrices.reshape(every_device_list, WEIGHT_SLOTS, INTERSECT_WIDTH, INTERSECT_WIDTH)
    tables = links.transpose(1, 0, 2, 3)
    offsets = (jnp.arange(every_device_list, dtype=jnp.int32) * NB)[:, None]

    def add_source(accumulated, entry):
        source_rows, source_weights, device_link_table = entry
        source_block = jnp.clip(device_link_table[0], 0, NB - 1).reshape(-1).astype(jnp.int32)
        target_block = (offsets + jnp.clip(device_link_table[1], 0, NB - 1)).reshape(-1).astype(jnp.int32)
        matrix_slot_index = jnp.clip(device_link_table[2], 0, WEIGHT_SLOTS - 1).reshape(-1).astype(jnp.int32)
        is_live = (device_link_table[0] >= 0).reshape(-1)
        message = jnp.einsum("efb,ebc->efc", source_rows[source_block], source_weights[matrix_slot_index], precision=highest)
        message = jnp.where(is_live[:, None, None], message, jnp.zeros_like(message))
        return accumulated.at[target_block].add(message), None

    start = jnp.zeros((every_device_list * NB, NF, INTERSECT_WIDTH), jnp.float32)
    accumulated, unused = lax.scan(add_source, start, (blocks, weight_entries, tables))
    forcing_next = accumulated.reshape(every_device_list, NB, NF, INTERSECT_WIDTH).transpose(2, 0, 1, 3).reshape(NF, every_device_list * NB * INTERSECT_WIDTH)

    forcing_term = jnp.einsum("slf,fsc->lsc", inject, forcing.reshape(NF, N_COMP, cycle_len), precision=highest) * wet_cells * DT
    mixing = diffuse.reshape(1, N_COMP, cycle_len)
    counts = substeps.reshape(1, N_COMP, cycle_len)
    for substep in range(SUBS):
        spread_term = jnp.roll(field, 1, axis=2) + jnp.roll(field, -1, axis=2) - 2.0 * field
        tendency = jnp.einsum("slm,msc->lsc", vertical, field, precision=highest)
        updated = field + mixing * spread_term + DT * tendency + forcing_term
        field = jnp.where(counts > substep, updated, field)
    return field.reshape(LEV, N_COMP * cycle_len), forcing_next
```

```python
import functools

import jax
import jax.numpy as jnp
from jax import lax
from jax.experimental import pallas as pl
from jax.experimental.pallas import tpu as pltpu
from jax.sharding import PartitionSpec as P

SUBS = 4
DT = 0.25
LANES = 128
WIDE = 256
STRIP = 512
LEAD = 2 * STRIP
GROUP = 8
PAD_ROWS = 80
CHUNKS = 4
MESH = pl.DeviceIdType.MESH
F32 = jnp.float32
BF16 = jnp.bfloat16


def high_low(x):
    high = x.astype(BF16)
    return high, (x - high.astype(F32)).astype(BF16)


def stack_left(scratch, parts):
    scratch[...] = jnp.zeros_like(scratch)
    for at, matrix in parts:
        high = matrix.astype(BF16).astype(F32)
        size = matrix.shape[1]
        for k, value in enumerate((high, high, matrix - high)):
            scratch[:, k * PAD_ROWS + at : k * PAD_ROWS + at + size] = value
    return scratch[...].astype(BF16)[:, : 3 * PAD_ROWS]


def second_difference(scratch):
    apart = lax.broadcasted_iota(jnp.int32, (WIDE, WIDE), 0) - lax.broadcasted_iota(
        jnp.int32, (WIDE, WIDE), 1
    )
    second = jnp.where(apart == 0, -2.0, jnp.where(jnp.abs(apart) == 1, 1.0, 0.0)).astype(BF16)
    scratch[0:WIDE] = second
    scratch[WIDE : 2 * WIDE] = second


def sweep(columns, chain, force, mix, sub, left_b, second):
    levels = chain[1].shape[0]
    blocks = columns // STRIP
    start = LEAD // STRIP
    lane = lax.broadcasted_iota(jnp.int32, (levels, LANES), 1)
    at_first = lane == 0
    at_last = lane == LANES - 1

    def place(b):
        base = b * STRIP
        return base if isinstance(b, int) else pl.multiple_of(base, STRIP)

    def take(j, b, shift, size):
        if j == 0:
            at = b * (STRIP // LANES) + shift // LANES
            return jnp.concatenate(
                [chain[0][:, at + u].reshape(levels, LANES) for u in range(size // LANES)], axis=1
            )
        return chain[j][:, pl.ds(place(b) + shift, size)]

    def compute(j, b):
        here = pl.ds(place(b), STRIP)
        x = take(j, b, 0, STRIP)
        high, low = high_low(jnp.concatenate([x, force[:, here]], axis=0))
        change = jnp.dot(
            left_b, jnp.concatenate([high, low, high], axis=0), preferred_element_type=F32
        )
        cuts = [slice(t * WIDE, (t + 1) * WIDE) for t in range(STRIP // WIDE)]
        lhs = jnp.concatenate(
            [jnp.concatenate([high[:, c], low[:, c]], axis=1) for c in cuts], axis=0
        )
        bent = jnp.dot(lhs, second[...], preferred_element_type=F32)
        lap = []
        for t in range(STRIP // WIDE):
            before = take(j, b, t * WIDE - LANES, LANES)
            after = take(j, b, (t + 1) * WIDE, LANES)
            own = bent[t * PAD_ROWS : t * PAD_ROWS + levels]
            lap.append(own[:, 0:LANES] + jnp.where(at_first, pltpu.roll(before, 1, axis=1), 0.0))
            lap.append(
                own[:, LANES:WIDE] + jnp.where(at_last, pltpu.roll(after, LANES - 1, axis=1), 0.0)
            )
        new = mix[:, here] * jnp.concatenate(lap, axis=1) + change
        if j > 0:
            new = jnp.where(sub[:, here] > j, new, x)
        return new

    def keep(j, b, new):
        if j < SUBS - 1:
            chain[j + 1][:, pl.ds(place(b), STRIP)] = new
        else:
            chain[SUBS][:, pl.ds(place(b - start), STRIP)] = new

    def advance_all(i, subs):
        for j in reversed(subs):
            keep(j, i - 2 * j, compute(j, i - 2 * j))

    low_b, high_b = start - 1, start + blocks

    def valid(i, j):
        b = i - 2 * j
        if j == SUBS - 1:
            return start <= b < start + blocks
        return low_b <= b <= high_b

    body_from = low_b + 2 * (SUBS - 1) + 1
    body_to = high_b + 1
    last = start + blocks - 1 + 2 * (SUBS - 1)
    for i in range(low_b, body_from):
        advance_all(i, [j for j in range(SUBS) if valid(i, j)])

    def body(i, carry):
        advance_all(i, list(range(SUBS)))
        return carry

    lax.fori_loop(body_from, body_to, body, 0)
    for i in range(body_to, last + 1):
        advance_all(i, [j for j in range(SUBS) if valid(i, j)])


def interval_kernel(
    comps,
    doms,
    links,
    state,
    forcing,
    vertical,
    inject,
    extract,
    diffuse,
    substeps,
    landmask,
    weights,
    out_v,
    arrived,
    targets,
    field_0,
    field_1,
    field_2,
    field_3,
    force_v,
    mix_v,
    sub_v,
    wet_v,
    vertical_v,
    inject_v,
    extract_v,
    weights_v,
    split_w,
    left_f,
    pick_f,
    second_b,
    msg,
    tgt,
    edge,
    halo,
    load_sem,
    small_sem,
    msg_send,
    msg_recv,
    tgt_send,
    tgt_recv,
    halo_send,
    halo_recv,
):
    levels, columns = vertical.shape[1], forcing.shape[1]
    fields = forcing.shape[0]
    comp = lax.axis_index("comp")
    dom = lax.axis_index("dom")
    me = comp * doms + dom
    air = (comps - 1) * doms
    is_air = comp < comps - 1
    count = jnp.where(is_air, doms, air)
    first = jnp.where(is_air, air, 0)
    right = lax.rem(dom + 1, doms)
    left = lax.rem(dom + doms - 1, doms)
    tail = LEAD + columns

    small = [
        pltpu.make_async_copy(src, dst, small_sem.at[k])
        for k, (src, dst) in enumerate(
            (
                (diffuse, mix_v.at[:, pl.ds(LEAD, columns)]),
                (substeps, sub_v.at[:, pl.ds(LEAD, columns)]),
                (landmask.at[0], wet_v),
                (forcing, force_v.at[:, pl.ds(LEAD, columns)]),
                (vertical.at[0], vertical_v),
                (inject.at[0], inject_v),
                (extract.at[0], extract_v),
                (weights, weights_v),
            )
        )
    ]
    chunk = columns // LANES // CHUNKS
    load = [
        pltpu.make_async_copy(
            state.at[:, pl.ds(c * chunk, chunk)],
            field_0.at[:, pl.ds(LEAD // LANES + c * chunk, chunk)],
            load_sem.at[c],
        )
        for c in range(CHUNKS)
    ]
    for copy in small[:4] + [load[0], load[-1]] + small[4:] + load[1:-1]:
        copy.start()

    barrier = pltpu.get_barrier_semaphore()
    for side in (left, right):
        pl.semaphore_signal(barrier, inc=1, device_id=(comp, side), device_id_type=MESH)

    def greet(p, carry):
        peer = first + p
        pl.semaphore_signal(
            barrier, inc=1, device_id=(peer // doms, peer % doms), device_id_type=MESH
        )
        return carry

    lax.fori_loop(0, count, greet, 0)

    second_difference(second_b)
    for copy in small[:4] + [load[0], load[-1]]:
        copy.wait()
    for t in range(columns // LANES):
        there = slice(LEAD + t * LANES, LEAD + (t + 1) * LANES)
        force_v[:, there] = force_v[:, there] * wet_v[t].astype(F32)
    for k, at in enumerate((tail - LANES, LEAD)):
        there = slice(at, at + LANES)
        edge[k, 0:levels] = field_0[:, at // LANES].reshape(levels, LANES)
        edge[k, levels : levels + 8] = force_v[:, there]
        edge[k, levels + 8 : levels + 16] = jnp.broadcast_to(mix_v[:, there], (8, LANES))
        edge[k, levels + 16 : levels + 24] = jnp.broadcast_to(
            sub_v[:, there].astype(F32), (8, LANES)
        )
    pl.semaphore_wait(barrier, count + 2)
    sides = [
        pltpu.make_async_remote_copy(
            src_ref=edge.at[k],
            dst_ref=halo.at[k],
            send_sem=halo_send.at[k],
            recv_sem=halo_recv.at[k],
            device_id=(comp, side),
            device_id_type=MESH,
        )
        for k, side in enumerate((right, left))
    ]
    for copy in sides:
        copy.start()

    for copy in small[4:]:
        copy.wait()
    pick_b = stack_left(pick_f, ((0, extract_v[...]),))
    eye = (
        lax.broadcasted_iota(jnp.int32, (levels, levels), 0)
        == lax.broadcasted_iota(jnp.int32, (levels, levels), 1)
    ).astype(F32)
    left_b = stack_left(
        left_f,
        (
            (0, vertical_v[...] * DT + eye),
            (levels, jnp.transpose(inject_v[...])[0:levels] * DT),
        ),
    )

    def split(s, carry):
        high, low = high_low(weights_v[s])
        split_w[s, 0:LANES] = high
        split_w[s, LANES:WIDE] = low
        return carry

    lax.fori_loop(0, weights_v.shape[0], split, 0, unroll=4)
    for copy in load[1:-1]:
        copy.wait()

    def send(p):
        peer = first + p
        spot = (peer // doms, peer % doms)
        return (
            pltpu.make_async_remote_copy(
                src_ref=msg.at[p],
                dst_ref=arrived.at[me],
                send_sem=msg_send.at[p],
                recv_sem=msg_recv.at[me],
                device_id=spot,
                device_id_type=MESH,
            ),
            pltpu.make_async_remote_copy(
                src_ref=tgt.at[p],
                dst_ref=targets.at[me],
                send_sem=tgt_send.at[p],
                recv_sem=tgt_recv.at[me],
                device_id=spot,
                device_id_type=MESH,
            ),
        )

    lane = lax.broadcasted_iota(jnp.int32, (1, LANES), 1)
    blank = jnp.zeros((PAD_ROWS - levels, LANES), F32)

    def group(step, carry):
        rows = []
        for q in range(GROUP):
            peer = first + step * GROUP + q
            for k in range(2):
                block = jnp.maximum(links[0, 0, k, peer], 0)
                x = field_0[:, LEAD // LANES + block].reshape(levels, LANES)
                wet = wet_v[block]
                high, low = high_low(jnp.concatenate([x, blank], axis=0))
                rows.append((jnp.concatenate([high, low, high], axis=0), wet))
        outs = []
        for m in range(0, 2 * GROUP, 2):
            both = jnp.dot(
                pick_b,
                jnp.concatenate([rows[m][0], rows[m + 1][0]], axis=1),
                preferred_element_type=F32,
            )
            for k in range(2):
                r = both[:, k * LANES : (k + 1) * LANES] * rows[m + k][1].astype(F32)
                high = r.astype(BF16).astype(F32)
                low = r - high
                top = jnp.concatenate([high, high], axis=1)
                bottom = jnp.concatenate([low, jnp.zeros_like(low)], axis=1)
                lhs = jnp.concatenate([top, bottom], axis=0).astype(BF16)
                slot = jnp.maximum(links[2, 0, k, first + step * GROUP + m // 2], 0)
                out = jnp.dot(lhs, split_w[slot], preferred_element_type=F32)
                outs.append(out[0:8] + out[8:16])
        for q in range(GROUP):
            p = step * GROUP + q
            peer = first + p
            msg[p] = jnp.concatenate(outs[2 * q : 2 * q + 2], axis=0)
            t0 = jnp.where(lane == 0, links[1, 0, 0, peer], -1)
            tgt[p] = jnp.where(lane == 1, links[1, 0, 1, peer], t0)
        for q in range(GROUP):
            for copy in send(step * GROUP + q):
                copy.start()
        return carry

    lax.fori_loop(0, count // GROUP, group, 0)

    for copy in sides:
        copy.wait()
    for k, at in enumerate((LEAD - LANES, tail)):
        there = slice(at, at + LANES)
        field_0[:, at // LANES] = halo[k, 0:levels].reshape(levels // 8, 8, LANES)
        force_v[:, there] = halo[k, levels : levels + 8]
        mix_v[:, there] = halo[k, levels + 8 : levels + 9]
        sub_v[:, there] = halo[k, levels + 16 : levels + 17].astype(jnp.int32)
    for base, size in ((0, LEAD - LANES), (tail + LANES, LEAD - LANES)):
        field_0[:, base // LANES : (base + size) // LANES] = jnp.zeros(
            (levels // 8, size // LANES, 8, LANES), F32
        )
        force_v[:, base : base + size] = jnp.zeros((fields, size), F32)
        mix_v[:, base : base + size] = jnp.zeros((1, size), F32)
        sub_v[:, base : base + size] = jnp.zeros((1, size), jnp.int32)
    for field in (field_1, field_2, field_3):
        for at in (STRIP - LANES, tail + STRIP):
            field[:, at : at + LANES] = jnp.zeros((levels, LANES), F32)

    sweep(
        columns,
        (field_0, field_1, field_2, field_3, out_v),
        force_v,
        mix_v,
        sub_v,
        left_b,
        second_b,
    )

    def finish(p, carry):
        for copy in send(p):
            copy.wait_send()
        g = first + p
        pltpu.make_async_copy(arrived.at[g], arrived.at[g], msg_recv.at[g]).wait()
        pltpu.make_async_copy(targets.at[g], targets.at[g], tgt_recv.at[g]).wait()
        return carry

    lax.fori_loop(0, count, finish, 0)


def interval(comps, doms, links, state, forcing, vertical, inject, extract, diffuse, substeps, landmask, weights):
    levels, columns = vertical.shape[1], forcing.shape[1]
    fields = forcing.shape[0]
    slots = weights.shape[0]
    devices = comps * doms
    peers = max(doms, devices - doms)
    width = columns + 2 * LEAD
    hbm = pl.BlockSpec(memory_space=pltpu.HBM)
    vmem = pl.BlockSpec(memory_space=pltpu.VMEM)
    edge_rows = levels + 24
    return pl.pallas_call(
        functools.partial(interval_kernel, comps, doms),
        out_shape=(
            pltpu.VMEM((levels, columns), F32),
            jax.ShapeDtypeStruct((devices, 2 * fields, LANES), F32),
            jax.ShapeDtypeStruct((devices, 1, LANES), jnp.int32),
        ),
        in_specs=[pl.BlockSpec(memory_space=pltpu.SMEM)] + [hbm] * 9,
        out_specs=(vmem, hbm, hbm),
        scratch_shapes=[
            pltpu.VMEM((levels // 8, width // LANES, 8, LANES), F32),
            pltpu.VMEM((levels, width), F32),
            pltpu.VMEM((levels, width), F32),
            pltpu.VMEM((levels, width), F32),
            pltpu.VMEM((fields, width), F32),
            pltpu.VMEM((1, width), F32),
            pltpu.VMEM((1, width), jnp.int32),
            pltpu.VMEM((columns // LANES, 1, LANES), jnp.int32),
            pltpu.VMEM((levels, levels), F32),
            pltpu.VMEM((fields, levels), F32),
            pltpu.VMEM((fields, levels), F32),
            pltpu.VMEM(weights.shape, F32),
            pltpu.VMEM((slots, WIDE, LANES), BF16),
            pltpu.VMEM((levels, WIDE), F32),
            pltpu.VMEM((fields, WIDE), F32),
            pltpu.VMEM((2 * WIDE, WIDE), BF16),
            pltpu.VMEM((peers, 2 * fields, LANES), F32),
            pltpu.VMEM((peers, 1, LANES), jnp.int32),
            pltpu.VMEM((2, edge_rows, LANES), F32),
            pltpu.VMEM((2, edge_rows, LANES), F32),
            pltpu.SemaphoreType.DMA((CHUNKS,)),
            pltpu.SemaphoreType.DMA((8,)),
            pltpu.SemaphoreType.DMA((peers,)),
            pltpu.SemaphoreType.DMA((devices,)),
            pltpu.SemaphoreType.DMA((peers,)),
            pltpu.SemaphoreType.DMA((devices,)),
            pltpu.SemaphoreType.DMA((2,)),
            pltpu.SemaphoreType.DMA((2,)),
        ],
        compiler_params=pltpu.CompilerParams(
            collective_id=0, has_side_effects=True, vmem_limit_bytes=46 << 20
        ),
        name="interval",
    )(
        links,
        *(
            pltpu.with_memory_space_constraint(a, pltpu.HBM)
            for a in (
                state, forcing, vertical, inject, extract, diffuse, substeps, landmask, weights
            )
        )
    )


def deliver_kernel(
    comps, doms, targets, arrived, result, state_next, forcing_next, targets_s, arrived_v, next_v, sems
):
    columns = result.shape[1]
    chunk = columns // CHUNKS
    get_targets = pltpu.make_async_copy(targets, targets_s, sems.at[0])
    get_arrived = pltpu.make_async_copy(arrived, arrived_v, sems.at[1])
    get_targets.start()
    get_arrived.start()
    store = [
        pltpu.make_async_copy(
            result.at[:, pl.ds(c * chunk, chunk)],
            state_next.at[:, pl.ds(c * chunk, chunk)],
            sems.at[3 + c],
        )
        for c in range(CHUNKS)
    ]
    for copy in store:
        copy.start()
    next_v[...] = jnp.zeros_like(next_v)
    air = (comps - 1) * doms
    is_air = lax.axis_index("comp") < comps - 1
    count = jnp.where(is_air, doms, air)
    first = jnp.where(is_air, air, 0)
    get_targets.wait()
    get_arrived.wait()

    def scatter(p, carry):
        for k in range(2):
            t = targets_s[first + p, 0, k]
            there = pl.ds(pl.multiple_of(jnp.maximum(t, 0) * LANES, LANES), LANES)
            part = arrived_v[first + p, k * 8 : (k + 1) * 8]
            next_v[:, there] += jnp.where(t >= 0, part, jnp.zeros_like(part))
        return carry

    lax.fori_loop(0, count, scatter, 0)
    store_next = pltpu.make_async_copy(next_v, forcing_next, sems.at[2])
    store_next.start()
    for copy in store:
        copy.wait()
    store_next.wait()


def deliver(comps, doms, targets, arrived, result, fields):
    hbm = pl.BlockSpec(memory_space=pltpu.HBM)
    vmem = pl.BlockSpec(memory_space=pltpu.VMEM)
    columns = result.shape[1]
    return pl.pallas_call(
        functools.partial(deliver_kernel, comps, doms),
        out_shape=(
            jax.ShapeDtypeStruct(result.shape, F32),
            jax.ShapeDtypeStruct((fields, columns), F32),
        ),
        in_specs=[hbm, hbm, vmem],
        out_specs=(hbm, hbm),
        scratch_shapes=[
            pltpu.SMEM(targets.shape, jnp.int32),
            pltpu.VMEM(arrived.shape, F32),
            pltpu.VMEM((fields, columns), F32),
            pltpu.SemaphoreType.DMA((3 + CHUNKS,)),
        ],
        compiler_params=pltpu.CompilerParams(vmem_limit_bytes=8 << 20),
        name="deliver",
    )(targets, arrived, pltpu.with_memory_space_constraint(result, pltpu.VMEM))


def solution(mesh):
    comps, doms = mesh.shape["comp"], mesh.shape["dom"]

    def local(state, forcing, vertical, inject, extract, diffuse, substeps, landmask, links, weights):
        levels, columns = state.shape
        tiles = state.reshape(levels // 8, 8, columns // LANES, LANES).swapaxes(1, 2)
        result, arrived, targets = interval(
            comps,
            doms,
            links.swapaxes(2, 3),
            tiles,
            forcing,
            vertical,
            inject.swapaxes(1, 2),
            extract,
            diffuse.reshape(1, -1),
            substeps.reshape(1, -1),
            landmask.reshape(1, -1, 1, LANES),
            weights,
        )
        return deliver(comps, doms, targets, arrived, result, forcing.shape[0])

    return jax.shard_map(
        local,
        mesh=mesh,
        in_specs=(
            P(None, ("comp", "dom")),
            P(None, ("comp", "dom")),
            P("comp", None, None),
            P("comp", None, None),
            P("comp", None, None),
            P(("comp", "dom")),
            P(("comp", "dom")),
            P(("comp", "dom")),
            P(None, ("comp", "dom"), None, None),
            P(("comp", "dom"), None, None),
        ),
        out_specs=(P(None, ("comp", "dom")), P(None, ("comp", "dom"))),
        check_vma=False,
    )
```

```python
import functools

import jax
import jax.numpy as jnp
from jax import lax
from jax.experimental import pallas as pl
from jax.experimental.pallas import tpu as pltpu
from jax.sharding import PartitionSpec as P

SUBS = 4
DT = 0.25
LANES = 128
WIDE = 256
STRIP = 512
LEAD = STRIP
EXTRA = 3
SEND_AT = 14
GROUP = 8
PAD_ROWS = 80
CHUNKS = 4
MESH = pl.DeviceIdType.MESH
F32 = jnp.float32
BF16 = jnp.bfloat16


def high_low(x):
    high = x.astype(BF16)
    return high, (x - high.astype(F32)).astype(BF16)


def stack_left(scratch, parts):
    scratch[...] = jnp.zeros_like(scratch)
    for at, matrix in parts:
        high = matrix.astype(BF16).astype(F32)
        size = matrix.shape[1]
        for k, value in enumerate((high, high, matrix - high)):
            scratch[:, k * PAD_ROWS + at : k * PAD_ROWS + at + size] = value
    return scratch[...].astype(BF16)[:, : 3 * PAD_ROWS]


def second_difference(scratch):
    apart = lax.broadcasted_iota(jnp.int32, (WIDE, WIDE), 0) - lax.broadcasted_iota(
        jnp.int32, (WIDE, WIDE), 1
    )
    second = jnp.where(apart == 0, -2.0, jnp.where(jnp.abs(apart) == 1, 1.0, 0.0)).astype(BF16)
    scratch[0:WIDE] = second
    scratch[WIDE : 2 * WIDE] = second


def sweep(columns, chain, force, mix, sub, left_b, second, before):
    levels = chain[1].shape[0]
    blocks = columns // STRIP
    start = LEAD // STRIP
    lane = lax.broadcasted_iota(jnp.int32, (levels, LANES), 1)
    at_first = lane == 0
    at_last = lane == LANES - 1

    def place(b):
        base = b * STRIP
        return base if isinstance(b, int) else pl.multiple_of(base, STRIP)

    def take(j, b, shift, size):
        if j == 0:
            at = b * (STRIP // LANES) + shift // LANES
            return jnp.concatenate(
                [chain[0][:, at + u].reshape(levels, LANES) for u in range(size // LANES)], axis=1
            )
        return chain[j][:, pl.ds(place(b) + shift, size)]

    def compute(j, b):
        here = pl.ds(place(b), STRIP)
        x = take(j, b, 0, STRIP)
        high, low = high_low(jnp.concatenate([x, force[:, here]], axis=0))
        change = jnp.dot(
            left_b, jnp.concatenate([high, low, high], axis=0), preferred_element_type=F32
        )
        cuts = [slice(t * WIDE, (t + 1) * WIDE) for t in range(STRIP // WIDE)]
        lhs = jnp.concatenate(
            [jnp.concatenate([high[:, c], low[:, c]], axis=1) for c in cuts], axis=0
        )
        bent = jnp.dot(lhs, second[...], preferred_element_type=F32)
        lap = []
        for t in range(STRIP // WIDE):
            prior = take(j, b, t * WIDE - LANES, LANES)
            after = take(j, b, (t + 1) * WIDE, LANES)
            own = bent[t * PAD_ROWS : t * PAD_ROWS + levels]
            lap.append(own[:, 0:LANES] + jnp.where(at_first, pltpu.roll(prior, 1, axis=1), 0.0))
            lap.append(
                own[:, LANES:WIDE] + jnp.where(at_last, pltpu.roll(after, LANES - 1, axis=1), 0.0)
            )
        new = mix[:, here] * jnp.concatenate(lap, axis=1) + change
        if j > 0:
            new = jnp.where(sub[:, here] > j, new, x)
        return new

    def keep(j, b, new):
        if j < SUBS - 1:
            chain[j + 1][:, pl.ds(place(b), STRIP)] = new
        else:
            at = b - start
            if isinstance(b, int):
                at %= blocks + 1
            chain[SUBS][:, pl.ds(place(at), STRIP)] = new

    def advance_all(i, subs):
        for j in reversed(subs):
            keep(j, i - 2 * j, compute(j, i - 2 * j))

    lag = 2 * (SUBS - 1)

    def valid(i, j):
        b = i - 2 * j - start
        if j == SUBS - 1:
            return 1 <= b < blocks or b == blocks + 1
        return 0 <= b <= blocks + 2

    def body(i, carry):
        before(i - start)
        advance_all(i, list(range(SUBS)))
        return carry

    body_from, body_to = start + lag + 1, start + blocks + EXTRA
    for i in range(start, body_from):
        advance_all(i, [j for j in range(SUBS) if valid(i, j)])
    lax.fori_loop(body_from, body_to, body, 0)
    for i in range(body_to, start + blocks + 2 + lag):
        advance_all(i, [j for j in range(SUBS) if valid(i, j)])


def interval_kernel(
    comps,
    doms,
    links,
    state,
    forcing,
    vertical,
    inject,
    extract,
    diffuse,
    substeps,
    landmask,
    weights,
    out_v,
    arrived,
    targets,
    field_0,
    field_1,
    field_2,
    field_3,
    force_v,
    mix_v,
    sub_v,
    wet_v,
    vertical_v,
    inject_v,
    extract_v,
    weights_v,
    split_w,
    left_f,
    pick_f,
    second_b,
    msg,
    tgt,
    edge,
    halo,
    load_sem,
    small_sem,
    msg_send,
    msg_recv,
    tgt_send,
    tgt_recv,
    halo_send,
    halo_recv,
):
    levels, columns = vertical.shape[1], forcing.shape[1]
    fields = forcing.shape[0]
    comp = lax.axis_index("comp")
    dom = lax.axis_index("dom")
    me = comp * doms + dom
    air = (comps - 1) * doms
    is_air = comp < comps - 1
    count = jnp.where(is_air, doms, air)
    first = jnp.where(is_air, air, 0)
    right = lax.rem(dom + 1, doms)
    left = lax.rem(dom + doms - 1, doms)
    tail = LEAD + columns

    again = tail + STRIP
    small = [
        pltpu.make_async_copy(src, dst, small_sem.at[k])
        for k, (src, dst) in enumerate(
            (
                (vertical.at[0], vertical_v),
                (inject.at[0], inject_v),
                (diffuse, mix_v.at[:, pl.ds(LEAD, columns)]),
                (substeps, sub_v.at[:, pl.ds(LEAD, columns)]),
                (landmask.at[0], wet_v),
                (forcing, force_v.at[:, pl.ds(LEAD, columns)]),
                (extract.at[0], extract_v),
                (weights, weights_v),
                (state.at[:, pl.ds(0, 2 * STRIP // LANES)], field_0.at[:, pl.ds(again // LANES, 2 * STRIP // LANES)]),
            )
        )
    ]
    chunk = columns // LANES // CHUNKS

    def load(c):
        return pltpu.make_async_copy(
            state.at[:, pl.ds(c * chunk, chunk)],
            field_0.at[:, pl.ds(LEAD // LANES + c * chunk, chunk)],
            load_sem.at[c],
        )

    for copy in small[:6]:
        copy.start()
    for c in range(CHUNKS):
        load(c).start()
    for copy in small[6:]:
        copy.start()

    barrier = pltpu.get_barrier_semaphore()
    for side in (left, right):
        pl.semaphore_signal(barrier, inc=1, device_id=(comp, side), device_id_type=MESH)

    def greet(p, carry):
        peer = first + p
        pl.semaphore_signal(
            barrier, inc=1, device_id=(peer // doms, peer % doms), device_id_type=MESH
        )
        return carry

    lax.fori_loop(0, count, greet, 0)

    second_difference(second_b)
    end = again + 2 * STRIP
    for field in (field_1, field_2, field_3):
        for at in (LEAD - LANES, end):
            field[:, at : at + LANES] = jnp.zeros((levels, LANES), F32)
    for at, size in ((LEAD - LANES, LANES), (tail + LANES, STRIP - 2 * LANES), (end, LANES)):
        field_0[:, at // LANES : (at + size) // LANES] = jnp.zeros(
            (levels // 8, size // LANES, 8, LANES), F32
        )
    here = slice(tail, tail + STRIP)
    force_v[:, here] = jnp.zeros((fields, STRIP), F32)
    mix_v[:, here] = jnp.zeros((1, STRIP), F32)
    sub_v[:, here] = jnp.zeros((1, STRIP), jnp.int32)
    for copy in small[:6]:
        copy.wait()
    for t in range(columns // LANES):
        there = slice(LEAD + t * LANES, LEAD + (t + 1) * LANES)
        force_v[:, there] = force_v[:, there] * wet_v[t].astype(F32)
    for ref in (force_v, mix_v, sub_v):
        ref[:, again:end] = ref[:, LEAD : LEAD + 2 * STRIP]
    eye = (
        lax.broadcasted_iota(jnp.int32, (levels, levels), 0)
        == lax.broadcasted_iota(jnp.int32, (levels, levels), 1)
    ).astype(F32)
    left_b = stack_left(
        left_f,
        (
            (0, vertical_v[...] * DT + eye),
            (levels, jnp.transpose(inject_v[...])[0:levels] * DT),
        ),
    )
    sides = [
        pltpu.make_async_remote_copy(
            src_ref=edge.at[k],
            dst_ref=halo.at[k],
            send_sem=halo_send.at[k],
            recv_sem=halo_recv.at[k],
            device_id=(comp, side),
            device_id_type=MESH,
        )
        for k, side in enumerate((right, left))
    ]

    def send_sides():
        for k, at in enumerate((tail - LANES, LEAD)):
            there = slice(at, at + LANES)
            edge[k, 0:levels] = field_0[:, at // LANES].reshape(levels, LANES)
            edge[k, levels : levels + 8] = force_v[:, there]
            edge[k, levels + 8 : levels + 16] = jnp.broadcast_to(mix_v[:, there], (8, LANES))
            edge[k, levels + 16 : levels + 24] = jnp.broadcast_to(
                sub_v[:, there].astype(F32), (8, LANES)
            )
        for copy in sides:
            copy.start()

    def take_sides():
        for copy in sides:
            copy.wait()
        for k, at in enumerate((tail + STRIP - LANES, tail)):
            there = slice(at, at + LANES)
            field_0[:, at // LANES] = halo[k, 0:levels].reshape(levels // 8, 8, LANES)
            force_v[:, there] = halo[k, levels : levels + 8]
            mix_v[:, there] = halo[k, levels + 8 : levels + 9]
            sub_v[:, there] = halo[k, levels + 16 : levels + 17].astype(jnp.int32)

    def split(s, carry):
        high, low = high_low(weights_v[s])
        split_w[s, 0:LANES] = high
        split_w[s, LANES:WIDE] = low
        return carry

    def send(p):
        peer = first + p
        spot = (peer // doms, peer % doms)
        return (
            pltpu.make_async_remote_copy(
                src_ref=msg.at[p],
                dst_ref=arrived.at[me],
                send_sem=msg_send.at[p],
                recv_sem=msg_recv.at[me],
                device_id=spot,
                device_id_type=MESH,
            ),
            pltpu.make_async_remote_copy(
                src_ref=tgt.at[p],
                dst_ref=targets.at[me],
                send_sem=tgt_send.at[p],
                recv_sem=tgt_recv.at[me],
                device_id=spot,
                device_id_type=MESH,
            ),
        )

    lane = lax.broadcasted_iota(jnp.int32, (1, LANES), 1)
    blank = jnp.zeros((PAD_ROWS - levels, LANES), F32)

    def group(step, pick_b):
        rows = []
        for q in range(GROUP):
            peer = first + step * GROUP + q
            for k in range(2):
                block = jnp.maximum(links[0, 0, k, peer], 0)
                x = field_0[:, LEAD // LANES + block].reshape(levels, LANES)
                wet = wet_v[block]
                high, low = high_low(jnp.concatenate([x, blank], axis=0))
                rows.append((jnp.concatenate([high, low, high], axis=0), wet))
        outs = []
        for m in range(0, 2 * GROUP, 2):
            both = jnp.dot(
                pick_b,
                jnp.concatenate([rows[m][0], rows[m + 1][0]], axis=1),
                preferred_element_type=F32,
            )
            for k in range(2):
                r = both[:, k * LANES : (k + 1) * LANES] * rows[m + k][1].astype(F32)
                high = r.astype(BF16).astype(F32)
                low = r - high
                top = jnp.concatenate([high, high], axis=1)
                bottom = jnp.concatenate([low, jnp.zeros_like(low)], axis=1)
                lhs = jnp.concatenate([top, bottom], axis=0).astype(BF16)
                slot = jnp.maximum(links[2, 0, k, first + step * GROUP + m // 2], 0)
                out = jnp.dot(lhs, split_w[slot], preferred_element_type=F32)
                outs.append(out[0:8] + out[8:16])
        for q in range(GROUP):
            p = step * GROUP + q
            peer = first + p
            msg[p] = jnp.concatenate(outs[2 * q : 2 * q + 2], axis=0)
            t0 = jnp.where(lane == 0, links[1, 0, 0, peer], -1)
            tgt[p] = jnp.where(lane == 1, links[1, 0, 1, peer], t0)
        for q in range(GROUP):
            for copy in send(step * GROUP + q):
                copy.start()
        return pick_b

    def send_all():
        for c in range(sent_with + 1, CHUNKS):
            load(c).wait()
        for copy in small[6:]:
            copy.wait()
        pl.semaphore_wait(barrier, count + 2)
        send_sides()
        pick_b = stack_left(pick_f, ((0, extract_v[...]),))
        lax.fori_loop(0, weights_v.shape[0], split, 0, unroll=4)
        lax.fori_loop(0, count // GROUP, group, pick_b)

    run = columns // STRIP // CHUNKS
    sent_with = SEND_AT // run

    def before(i):
        @pl.when(((i + 1) % run == 0) & (i + 1 < SEND_AT))
        def _():
            load((i + 1) // run).wait()

        @pl.when(i == SEND_AT)
        def _():
            send_all()

        @pl.when(i == columns // STRIP - 1)
        def _():
            take_sides()

    load(0).wait()
    sweep(
        columns,
        (field_0, field_1, field_2, field_3, out_v),
        force_v,
        mix_v,
        sub_v,
        left_b,
        second_b,
        before,
    )

    def finish(p, carry):
        for copy in send(p):
            copy.wait_send()
        g = first + p
        pltpu.make_async_copy(arrived.at[g], arrived.at[g], msg_recv.at[g]).wait()
        pltpu.make_async_copy(targets.at[g], targets.at[g], tgt_recv.at[g]).wait()
        return carry

    lax.fori_loop(0, count, finish, 0)


def interval(comps, doms, links, state, forcing, vertical, inject, extract, diffuse, substeps, landmask, weights):
    levels, columns = vertical.shape[1], forcing.shape[1]
    fields = forcing.shape[0]
    slots = weights.shape[0]
    devices = comps * doms
    peers = max(doms, devices - doms)
    width = LEAD + columns + EXTRA * STRIP + LANES
    hbm = pl.BlockSpec(memory_space=pltpu.HBM)
    vmem = pl.BlockSpec(memory_space=pltpu.VMEM)
    edge_rows = levels + 24
    return pl.pallas_call(
        functools.partial(interval_kernel, comps, doms),
        out_shape=(
            pltpu.VMEM((levels, columns), F32),
            jax.ShapeDtypeStruct((devices, 2 * fields, LANES), F32),
            jax.ShapeDtypeStruct((devices, 1, LANES), jnp.int32),
        ),
        in_specs=[pl.BlockSpec(memory_space=pltpu.SMEM)] + [hbm] * 9,
        out_specs=(vmem, hbm, hbm),
        scratch_shapes=[
            pltpu.VMEM((levels // 8, width // LANES, 8, LANES), F32),
            pltpu.VMEM((levels, width), F32),
            pltpu.VMEM((levels, width), F32),
            pltpu.VMEM((levels, width), F32),
            pltpu.VMEM((fields, width), F32),
            pltpu.VMEM((1, width), F32),
            pltpu.VMEM((1, width), jnp.int32),
            pltpu.VMEM((columns // LANES, 1, LANES), jnp.int32),
            pltpu.VMEM((levels, levels), F32),
            pltpu.VMEM((fields, levels), F32),
            pltpu.VMEM((fields, levels), F32),
            pltpu.VMEM(weights.shape, F32),
            pltpu.VMEM((slots, WIDE, LANES), BF16),
            pltpu.VMEM((levels, WIDE), F32),
            pltpu.VMEM((fields, WIDE), F32),
            pltpu.VMEM((2 * WIDE, WIDE), BF16),
            pltpu.VMEM((peers, 2 * fields, LANES), F32),
            pltpu.VMEM((peers, 1, LANES), jnp.int32),
            pltpu.VMEM((2, edge_rows, LANES), F32),
            pltpu.VMEM((2, edge_rows, LANES), F32),
            pltpu.SemaphoreType.DMA((CHUNKS,)),
            pltpu.SemaphoreType.DMA((9,)),
            pltpu.SemaphoreType.DMA((peers,)),
            pltpu.SemaphoreType.DMA((devices,)),
            pltpu.SemaphoreType.DMA((peers,)),
            pltpu.SemaphoreType.DMA((devices,)),
            pltpu.SemaphoreType.DMA((2,)),
            pltpu.SemaphoreType.DMA((2,)),
        ],
        compiler_params=pltpu.CompilerParams(
            collective_id=0, has_side_effects=True, vmem_limit_bytes=46 << 20
        ),
        name="interval",
    )(
        links,
        *(
            pltpu.with_memory_space_constraint(a, pltpu.HBM)
            for a in (
                state, forcing, vertical, inject, extract, diffuse, substeps, landmask, weights
            )
        )
    )


def deliver_kernel(
    comps, doms, targets, arrived, result, state_next, forcing_next, targets_s, arrived_v, next_v, sems
):
    columns = result.shape[1]
    chunk = columns // CHUNKS
    get_targets = pltpu.make_async_copy(targets, targets_s, sems.at[0])
    get_arrived = pltpu.make_async_copy(arrived, arrived_v, sems.at[1])
    get_targets.start()
    get_arrived.start()
    store = [
        pltpu.make_async_copy(
            result.at[:, pl.ds(c * chunk, chunk)],
            state_next.at[:, pl.ds(c * chunk, chunk)],
            sems.at[3 + c],
        )
        for c in range(CHUNKS)
    ]
    for copy in store:
        copy.start()
    next_v[...] = jnp.zeros_like(next_v)
    air = (comps - 1) * doms
    is_air = lax.axis_index("comp") < comps - 1
    count = jnp.where(is_air, doms, air)
    first = jnp.where(is_air, air, 0)
    get_targets.wait()
    get_arrived.wait()

    def scatter(p, carry):
        for k in range(2):
            t = targets_s[first + p, 0, k]
            there = pl.ds(pl.multiple_of(jnp.maximum(t, 0) * LANES, LANES), LANES)
            part = arrived_v[first + p, k * 8 : (k + 1) * 8]
            next_v[:, there] += jnp.where(t >= 0, part, jnp.zeros_like(part))
        return carry

    lax.fori_loop(0, count, scatter, 0)
    store_next = pltpu.make_async_copy(next_v, forcing_next, sems.at[2])
    store_next.start()
    for copy in store:
        copy.wait()
    store_next.wait()


def deliver(comps, doms, targets, arrived, result, fields):
    hbm = pl.BlockSpec(memory_space=pltpu.HBM)
    vmem = pl.BlockSpec(memory_space=pltpu.VMEM)
    columns = result.shape[1]
    return pl.pallas_call(
        functools.partial(deliver_kernel, comps, doms),
        out_shape=(
            jax.ShapeDtypeStruct(result.shape, F32),
            jax.ShapeDtypeStruct((fields, columns), F32),
        ),
        in_specs=[hbm, hbm, vmem],
        out_specs=(hbm, hbm),
        scratch_shapes=[
            pltpu.SMEM(targets.shape, jnp.int32),
            pltpu.VMEM(arrived.shape, F32),
            pltpu.VMEM((fields, columns), F32),
            pltpu.SemaphoreType.DMA((3 + CHUNKS,)),
        ],
        compiler_params=pltpu.CompilerParams(vmem_limit_bytes=8 << 20),
        name="deliver",
    )(targets, arrived, pltpu.with_memory_space_constraint(result, pltpu.VMEM))


def solution(mesh):
    comps, doms = mesh.shape["comp"], mesh.shape["dom"]

    def local(state, forcing, vertical, inject, extract, diffuse, substeps, landmask, links, weights):
        levels, columns = state.shape
        tiles = state.reshape(levels // 8, 8, columns // LANES, LANES).swapaxes(1, 2)
        result, arrived, targets = interval(
            comps,
            doms,
            links.swapaxes(2, 3),
            tiles,
            forcing,
            vertical,
            inject.swapaxes(1, 2),
            extract,
            diffuse.reshape(1, -1),
            substeps.reshape(1, -1),
            landmask.reshape(1, -1, 1, LANES),
            weights,
        )
        return deliver(comps, doms, targets, arrived, result, forcing.shape[0])

    return jax.shard_map(
        local,
        mesh=mesh,
        in_specs=(
            P(None, ("comp", "dom")),
            P(None, ("comp", "dom")),
            P("comp", None, None),
            P("comp", None, None),
            P("comp", None, None),
            P(("comp", "dom")),
            P(("comp", "dom")),
            P(("comp", "dom")),
            P(None, ("comp", "dom"), None, None),
            P(("comp", "dom"), None, None),
        ),
        out_specs=(P(None, ("comp", "dom")), P(None, ("comp", "dom"))),
        check_vma=False,
    )
```

```python
import functools

import jax
import jax.numpy as jnp
from jax import lax
from jax.experimental import pallas as pl
from jax.experimental.pallas import tpu as pltpu
from jax.sharding import PartitionSpec as P

SUBS = 4
DT = 0.25
LANES = 128
WIDE = 256
STEP = 16
BENT = 8
ENDS = 6
GROUP = 8
PAD_ROWS = 80
MESH = pl.DeviceIdType.MESH
F32 = jnp.float32
BF16 = jnp.bfloat16


def high_low(x):
    high = x.astype(BF16)
    return high, (x - high.astype(F32)).astype(BF16)


def stack_left(scratch, parts):
    scratch[...] = jnp.zeros_like(scratch)
    for at, matrix in parts:
        high = matrix.astype(BF16).astype(F32)
        size = matrix.shape[1]
        for k, value in enumerate((high, high, matrix - high)):
            scratch[:, k * PAD_ROWS + at : k * PAD_ROWS + at + size] = value
    return scratch[...].astype(BF16)[:, : 3 * PAD_ROWS]


def second_difference(scratch):
    apart = lax.broadcasted_iota(jnp.int32, (WIDE, WIDE), 0) - lax.broadcasted_iota(
        jnp.int32, (WIDE, WIDE), 1
    )
    second = jnp.where(apart == 0, -2.0, jnp.where(jnp.abs(apart) == 1, 1.0, 0.0)).astype(BF16)
    scratch[0:WIDE] = second
    scratch[WIDE : 2 * WIDE] = second


def stepper(force, mix, sub, left_b, second):
    levels = left_b.shape[0]
    groups = levels // 8
    lane = lax.broadcasted_iota(jnp.int32, (levels, LANES), 1)
    at_first = lane == 0
    at_last = lane == LANES - 1

    def step(src, dst, j, at, tiles, bent):
        def whole(t):
            return src[:, at + t].reshape(levels, LANES)

        here = pl.ds(at * LANES if isinstance(at, int) else pl.multiple_of(at * LANES, LANES), tiles * LANES)
        x = [whole(t) for t in range(tiles)]
        high, low = high_low(
            jnp.concatenate([jnp.concatenate(x, axis=1), force[:, here]], axis=0)
        )
        change = jnp.dot(
            left_b, jnp.concatenate([high, low, high], axis=0), preferred_element_type=F32
        )
        wide = []
        if bent:
            cuts = [slice(t * LANES, (t + 2) * LANES) for t in range(0, bent, 2)]
            lhs = jnp.concatenate(
                [jnp.concatenate([high[:, c], low[:, c]], axis=1) for c in cuts], axis=0
            )
            out = jnp.dot(lhs, second[...], preferred_element_type=F32)
            wide = [out[k * PAD_ROWS : k * PAD_ROWS + levels] for k in range(bent // 2)]
        turned = {}

        def turn(t, by):
            if (t, by) not in turned:
                value = x[t] if 0 <= t < tiles else whole(t)
                turned[t, by] = pltpu.roll(value, by % LANES, axis=1)
            return turned[t, by]

        d = mix[:, here]
        live = sub[:, here] > j
        for t in range(tiles):
            cut = slice(t * LANES, (t + 1) * LANES)
            if t < bent:
                own = wide[t // 2][:, (t % 2) * LANES : (t % 2 + 1) * LANES]
                if t % 2 == 0:
                    lap = own + jnp.where(at_first, turn(t - 1, 1), 0.0)
                else:
                    lap = own + jnp.where(at_last, turn(t + 1, -1), 0.0)
            else:
                prior = jnp.where(at_first, turn(t - 1, 1), turn(t, 1))
                after = jnp.where(at_last, turn(t + 1, -1), turn(t, -1))
                lap = (prior - x[t]) + (after - x[t])
            new = jnp.where(live[:, cut], d[:, cut] * lap + change[:, cut], x[t])
            dst[:, at + t] = new.reshape(groups, 8, LANES)

    return step


def interval_kernel(
    comps,
    doms,
    links,
    state,
    forcing,
    vertical,
    inject,
    extract,
    diffuse,
    substeps,
    landmask,
    weights,
    field_0,
    arrived,
    targets,
    field_1,
    end_0,
    end_1,
    end_force,
    end_mix,
    end_sub,
    links_s,
    force_v,
    mix_v,
    sub_v,
    wet_v,
    vertical_v,
    inject_v,
    extract_v,
    weights_v,
    split_w,
    left_f,
    pick_f,
    second_b,
    msg,
    tgt,
    edge,
    halo,
    load_sem,
    small_sem,
    msg_send,
    msg_recv,
    tgt_send,
    tgt_recv,
    halo_send,
    halo_recv,
):
    levels, columns = vertical.shape[1], forcing.shape[1]
    fields = forcing.shape[0]
    comp = lax.axis_index("comp")
    dom = lax.axis_index("dom")
    me = comp * doms + dom
    air = (comps - 1) * doms
    is_air = comp < comps - 1
    count = jnp.where(is_air, doms, air)
    first = jnp.where(is_air, air, 0)
    right = lax.rem(dom + 1, doms)
    left = lax.rem(dom + doms - 1, doms)
    tiles = columns // LANES
    chunks = tiles // STEP

    small = [
        pltpu.make_async_copy(src, dst, small_sem.at[k])
        for k, (src, dst) in enumerate(
            (
                (vertical.at[0], vertical_v),
                (inject.at[0], inject_v),
                (diffuse, mix_v.at[:, pl.ds(LANES, columns)]),
                (substeps, sub_v.at[:, pl.ds(LANES, columns)]),
                (landmask.at[0], wet_v),
                (forcing, force_v.at[:, pl.ds(LANES, columns)]),
                (extract.at[0], extract_v),
                (weights, weights_v),
                (links, links_s),
            )
        )
    ]
    def load(c):
        return pltpu.make_async_copy(
            state.at[:, pl.ds(c * STEP, STEP)],
            field_0.at[:, pl.ds(1 + c * STEP, STEP)],
            load_sem.at[c],
        )

    for copy in small[:6]:
        copy.start()
    for c in range(chunks):
        load(c).start()
    for copy in small[6:]:
        copy.start()

    barrier = pltpu.get_barrier_semaphore()
    for side in (left, right):
        pl.semaphore_signal(barrier, inc=1, device_id=(comp, side), device_id_type=MESH)

    def greet(p, carry):
        peer = first + p
        pl.semaphore_signal(
            barrier, inc=1, device_id=(peer // doms, peer % doms), device_id_type=MESH
        )
        return carry

    lax.fori_loop(0, count, greet, 0)

    second_difference(second_b)
    blank_tile = jnp.zeros((levels // 8, 8, LANES), F32)
    for field, outer in ((field_0, tiles + 1), (field_1, tiles + 1), (end_0, ENDS - 1), (end_1, ENDS - 1)):
        field[:, 0] = blank_tile
        field[:, outer] = blank_tile
    for copy in small[:6]:
        copy.wait()
    for t in range(tiles):
        there = slice(LANES + t * LANES, 2 * LANES + t * LANES)
        force_v[:, there] = force_v[:, there] * wet_v[t].astype(F32)
    eye = (
        lax.broadcasted_iota(jnp.int32, (levels, levels), 0)
        == lax.broadcasted_iota(jnp.int32, (levels, levels), 1)
    ).astype(F32)
    left_b = stack_left(
        left_f,
        (
            (0, vertical_v[...] * DT + eye),
            (levels, jnp.transpose(inject_v[...])[0:levels] * DT),
        ),
    )
    sides = [
        pltpu.make_async_remote_copy(
            src_ref=edge.at[k],
            dst_ref=halo.at[k],
            send_sem=halo_send.at[k],
            recv_sem=halo_recv.at[k],
            device_id=(comp, side),
            device_id_type=MESH,
        )
        for k, side in enumerate((right, left))
    ]

    def send_sides():
        for k, at in enumerate((tiles, 1)):
            there = slice(at * LANES, (at + 1) * LANES)
            edge[k, 0:levels] = field_0[:, at].reshape(levels, LANES)
            edge[k, levels : levels + 8] = force_v[:, there]
            edge[k, levels + 8 : levels + 16] = jnp.broadcast_to(mix_v[:, there], (8, LANES))
            edge[k, levels + 16 : levels + 24] = jnp.broadcast_to(
                sub_v[:, there].astype(F32), (8, LANES)
            )
        for copy in sides:
            copy.start()

    def take_sides():
        for copy in sides:
            copy.wait()
        for at, part in ((1, halo.at[0]), (2, edge.at[1]), (3, edge.at[0]), (4, halo.at[1])):
            there = slice(at * LANES, (at + 1) * LANES)
            end_0[:, at] = part[0:levels].reshape(levels // 8, 8, LANES)
            end_force[:, there] = part[levels : levels + 8]
            end_mix[:, there] = part[levels + 8 : levels + 9]
            end_sub[:, there] = part[levels + 16 : levels + 17].astype(jnp.int32)

    def split(s, carry):
        high, low = high_low(weights_v[s])
        split_w[s, 0:LANES] = high
        split_w[s, LANES:WIDE] = low
        return carry

    def send(p):
        peer = first + p
        spot = (peer // doms, peer % doms)
        return (
            pltpu.make_async_remote_copy(
                src_ref=msg.at[p],
                dst_ref=arrived.at[me],
                send_sem=msg_send.at[p],
                recv_sem=msg_recv.at[me],
                device_id=spot,
                device_id_type=MESH,
            ),
            pltpu.make_async_remote_copy(
                src_ref=tgt.at[p],
                dst_ref=targets.at[me],
                send_sem=tgt_send.at[p],
                recv_sem=tgt_recv.at[me],
                device_id=spot,
                device_id_type=MESH,
            ),
        )

    lane = lax.broadcasted_iota(jnp.int32, (1, LANES), 1)
    blank = jnp.zeros((PAD_ROWS - levels, LANES), F32)

    def group(step, pick_b):
        rows = []
        for q in range(GROUP):
            peer = first + step * GROUP + q
            for k in range(2):
                block = jnp.maximum(links_s[0, 0, k, peer], 0)
                x = field_0[:, 1 + block].reshape(levels, LANES)
                wet = wet_v[block]
                high, low = high_low(jnp.concatenate([x, blank], axis=0))
                rows.append((jnp.concatenate([high, low, high], axis=0), wet))
        outs = []
        for m in range(0, 2 * GROUP, 2):
            both = jnp.dot(
                pick_b,
                jnp.concatenate([rows[m][0], rows[m + 1][0]], axis=1),
                preferred_element_type=F32,
            )
            for k in range(2):
                r = both[:, k * LANES : (k + 1) * LANES] * rows[m + k][1].astype(F32)
                high = r.astype(BF16).astype(F32)
                low = r - high
                top = jnp.concatenate([high, high], axis=1)
                bottom = jnp.concatenate([low, jnp.zeros_like(low)], axis=1)
                lhs = jnp.concatenate([top, bottom], axis=0).astype(BF16)
                slot = jnp.maximum(links_s[2, 0, k, first + step * GROUP + m // 2], 0)
                out = jnp.dot(lhs, split_w[slot], preferred_element_type=F32)
                outs.append(out[0:8] + out[8:16])
        for q in range(GROUP):
            p = step * GROUP + q
            peer = first + p
            msg[p] = jnp.concatenate(outs[2 * q : 2 * q + 2], axis=0)
            t0 = jnp.where(lane == 0, links_s[1, 0, 0, peer], -1)
            tgt[p] = jnp.where(lane == 1, links_s[1, 0, 1, peer], t0)
        for q in range(GROUP):
            for copy in send(step * GROUP + q):
                copy.start()
        return pick_b

    def send_all():
        for copy in small[6:]:
            copy.wait()
        pl.semaphore_wait(barrier, count + 2)
        send_sides()
        pick_b = stack_left(pick_f, ((0, extract_v[...]),))
        lax.fori_loop(0, weights_v.shape[0], split, 0, unroll=4)
        lax.fori_loop(0, count // GROUP, group, pick_b)

    step = stepper(force_v, mix_v, sub_v, left_b, second_b)
    end_step = stepper(end_force, end_mix, end_sub, left_b, second_b)
    load(0).wait()

    def twice(pair, carry):
        def even(i, carry):
            @pl.when((pair == 0) & (i < chunks - 1))
            def _():
                load(i + 1).wait()

            step(field_0, field_1, 2 * pair, 1 + i * STEP, STEP, BENT)
            return carry

        def odd(i, carry):
            step(field_1, field_0, 2 * pair + 1, 1 + i * STEP, STEP, BENT)
            return carry

        lax.fori_loop(0, chunks, even, 0)

        @pl.when(pair == 0)
        def _():
            send_all()

        lax.fori_loop(0, chunks, odd, 0)
        return carry

    lax.fori_loop(0, SUBS // 2, twice, 0)
    take_sides()

    def end_twice(pair, carry):
        end_step(end_0, end_1, 2 * pair, 1, ENDS - 2, ENDS - 2)
        end_step(end_1, end_0, 2 * pair + 1, 1, ENDS - 2, ENDS - 2)
        return carry

    lax.fori_loop(0, SUBS // 2, end_twice, 0)
    near = lax.broadcasted_iota(jnp.int32, (levels // 8, 8, LANES), 2) < LANES // 2
    field_0[:, 1] = jnp.where(near, end_0[:, 2], field_0[:, 1])
    field_0[:, tiles] = jnp.where(near, field_0[:, tiles], end_0[:, 3])

    def finish(p, carry):
        for copy in send(p):
            copy.wait_send()
        g = first + p
        pltpu.make_async_copy(arrived.at[g], arrived.at[g], msg_recv.at[g]).wait()
        pltpu.make_async_copy(targets.at[g], targets.at[g], tgt_recv.at[g]).wait()
        return carry

    lax.fori_loop(0, count, finish, 0)


def interval(comps, doms, links, state, forcing, vertical, inject, extract, diffuse, substeps, landmask, weights):
    levels, columns = vertical.shape[1], forcing.shape[1]
    fields = forcing.shape[0]
    slots = weights.shape[0]
    devices = comps * doms
    peers = max(doms, devices - doms)
    width = columns + 2 * LANES
    stack = (levels // 8, width // LANES, 8, LANES)
    ends = (levels // 8, ENDS, 8, LANES)
    hbm = pl.BlockSpec(memory_space=pltpu.HBM)
    vmem = pl.BlockSpec(memory_space=pltpu.VMEM)
    edge_rows = levels + 24
    return pl.pallas_call(
        functools.partial(interval_kernel, comps, doms),
        out_shape=(
            pltpu.VMEM(stack, F32),
            jax.ShapeDtypeStruct((devices, 2 * fields, LANES), F32),
            jax.ShapeDtypeStruct((devices, 1, LANES), jnp.int32),
        ),
        in_specs=[hbm] * 10,
        out_specs=(vmem, hbm, hbm),
        scratch_shapes=[
            pltpu.VMEM(stack, F32),
            pltpu.VMEM(ends, F32),
            pltpu.VMEM(ends, F32),
            pltpu.VMEM((fields, ENDS * LANES), F32),
            pltpu.VMEM((1, ENDS * LANES), F32),
            pltpu.VMEM((1, ENDS * LANES), jnp.int32),
            pltpu.SMEM(links.shape, jnp.int32),
            pltpu.VMEM((fields, width), F32),
            pltpu.VMEM((1, width), F32),
            pltpu.VMEM((1, width), jnp.int32),
            pltpu.VMEM((columns // LANES, 1, LANES), jnp.int32),
            pltpu.VMEM((levels, levels), F32),
            pltpu.VMEM((fields, levels), F32),
            pltpu.VMEM((fields, levels), F32),
            pltpu.VMEM(weights.shape, F32),
            pltpu.VMEM((slots, WIDE, LANES), BF16),
            pltpu.VMEM((levels, WIDE), F32),
            pltpu.VMEM((fields, WIDE), F32),
            pltpu.VMEM((2 * WIDE, WIDE), BF16),
            pltpu.VMEM((peers, 2 * fields, LANES), F32),
            pltpu.VMEM((peers, 1, LANES), jnp.int32),
            pltpu.VMEM((2, edge_rows, LANES), F32),
            pltpu.VMEM((2, edge_rows, LANES), F32),
            pltpu.SemaphoreType.DMA((columns // LANES // STEP,)),
            pltpu.SemaphoreType.DMA((9,)),
            pltpu.SemaphoreType.DMA((peers,)),
            pltpu.SemaphoreType.DMA((devices,)),
            pltpu.SemaphoreType.DMA((peers,)),
            pltpu.SemaphoreType.DMA((devices,)),
            pltpu.SemaphoreType.DMA((2,)),
            pltpu.SemaphoreType.DMA((2,)),
        ],
        compiler_params=pltpu.CompilerParams(
            collective_id=0, has_side_effects=True, vmem_limit_bytes=40 << 20
        ),
        name="interval",
    )(
        *(
            pltpu.with_memory_space_constraint(a, pltpu.HBM)
            for a in (
                links, state, forcing, vertical, inject, extract, diffuse, substeps, landmask, weights
            )
        )
    )


def deliver_kernel(
    comps, doms, targets, arrived, result, state_next, forcing_next, targets_s, arrived_v, next_v, sems
):
    chunks = sems.shape[0] - 3
    chunk = state_next.shape[1] // chunks
    get_targets = pltpu.make_async_copy(targets, targets_s, sems.at[0])
    get_arrived = pltpu.make_async_copy(arrived, arrived_v, sems.at[1])
    get_targets.start()
    get_arrived.start()
    store = [
        pltpu.make_async_copy(
            result.at[:, pl.ds(1 + c * chunk, chunk)],
            state_next.at[:, pl.ds(c * chunk, chunk)],
            sems.at[3 + c],
        )
        for c in range(chunks)
    ]
    for copy in store:
        copy.start()
    next_v[...] = jnp.zeros_like(next_v)
    air = (comps - 1) * doms
    is_air = lax.axis_index("comp") < comps - 1
    count = jnp.where(is_air, doms, air)
    first = jnp.where(is_air, air, 0)
    get_targets.wait()
    get_arrived.wait()

    def scatter(p, carry):
        for k in range(2):
            t = targets_s[first + p, 0, k]
            there = pl.ds(pl.multiple_of(jnp.maximum(t, 0) * LANES, LANES), LANES)
            part = arrived_v[first + p, k * 8 : (k + 1) * 8]
            next_v[:, there] += jnp.where(t >= 0, part, jnp.zeros_like(part))
        return carry

    lax.fori_loop(0, count, scatter, 0)
    store_next = pltpu.make_async_copy(next_v, forcing_next, sems.at[2])
    store_next.start()
    for copy in store:
        copy.wait()
    store_next.wait()


def deliver(comps, doms, targets, arrived, result, fields):
    hbm = pl.BlockSpec(memory_space=pltpu.HBM)
    vmem = pl.BlockSpec(memory_space=pltpu.VMEM)
    groups, tiles = result.shape[0], result.shape[1] - 2
    columns = tiles * LANES
    return pl.pallas_call(
        functools.partial(deliver_kernel, comps, doms),
        out_shape=(
            jax.ShapeDtypeStruct((groups, tiles, 8, LANES), F32),
            jax.ShapeDtypeStruct((fields, columns), F32),
        ),
        in_specs=[hbm, hbm, vmem],
        out_specs=(hbm, hbm),
        scratch_shapes=[
            pltpu.SMEM(targets.shape, jnp.int32),
            pltpu.VMEM(arrived.shape, F32),
            pltpu.VMEM((fields, columns), F32),
            pltpu.SemaphoreType.DMA((3 + 4,)),
        ],
        compiler_params=pltpu.CompilerParams(vmem_limit_bytes=8 << 20),
        name="deliver",
    )(targets, arrived, pltpu.with_memory_space_constraint(result, pltpu.VMEM))


def solution(mesh):
    comps, doms = mesh.shape["comp"], mesh.shape["dom"]

    def local(state, forcing, vertical, inject, extract, diffuse, substeps, landmask, links, weights):
        levels, columns = state.shape
        tiles = state.reshape(levels // 8, 8, columns // LANES, LANES).swapaxes(1, 2)
        result, arrived, targets = interval(
            comps,
            doms,
            links.swapaxes(2, 3),
            tiles,
            forcing,
            vertical,
            inject.swapaxes(1, 2),
            extract,
            diffuse.reshape(1, -1),
            substeps.reshape(1, -1),
            landmask.reshape(1, -1, 1, LANES),
            weights,
        )
        new, forcing_next = deliver(comps, doms, targets, arrived, result, forcing.shape[0])
        return new.swapaxes(1, 2).reshape(state.shape), forcing_next

    return jax.shard_map(
        local,
        mesh=mesh,
        in_specs=(
            P(None, ("comp", "dom")),
            P(None, ("comp", "dom")),
            P("comp", None, None),
            P("comp", None, None),
            P("comp", None, None),
            P(("comp", "dom")),
            P(("comp", "dom")),
            P(("comp", "dom")),
            P(None, ("comp", "dom"), None, None),
            P(("comp", "dom"), None, None),
        ),
        out_specs=(P(None, ("comp", "dom")), P(None, ("comp", "dom"))),
        check_vma=False,
    )
```

```python
import functools
import math

import jax
import jax.numpy as jnp
from jax import lax
from jax.experimental import pallas as pl
from jax.experimental.pallas import tpu as pltpu
from jax.sharding import PartitionSpec as P

SUBS = 4
DT = 0.25
LANES = 128
WIDE = 256
STEP = 32
ENDS = 6
GROUP = 8
PAD_ROWS = 80
MESH = pl.DeviceIdType.MESH
F32 = jnp.float32
BF16 = jnp.bfloat16


def high_low(x):
    high = x.astype(BF16)
    return high, (x - high.astype(F32)).astype(BF16)


def stack_left(scratch, parts):
    scratch[...] = jnp.zeros_like(scratch)
    for at, matrix in parts:
        high = matrix.astype(BF16).astype(F32)
        size = matrix.shape[1]
        for k, value in enumerate((high, high, matrix - high)):
            scratch[:, k * PAD_ROWS + at : k * PAD_ROWS + at + size] = value
    return scratch[...].astype(BF16)[:, : 3 * PAD_ROWS]


def flip(dst, to, src, at, tiles):
    flat = [ref.reshape(math.prod(ref.shape[:-1]), LANES) for ref in (dst, src)]
    value = flat[1][pl.ds(at, tiles, stride=8), :]
    flat[0][pl.ds(to, tiles, stride=8), :] = jnp.transpose(value)


def substep(src, dst, at, tiles, force, mix, live, left_b):
    levels = left_b.shape[0]
    x = [src[:, at + t].reshape(levels, LANES) for t in range(-1, tiles + 1)]
    values = jnp.concatenate(x[1:-1], axis=1)
    high, low = high_low(
        jnp.concatenate([values, jnp.concatenate([force(t) for t in range(tiles)], axis=1)], axis=0)
    )
    change = jnp.dot(
        left_b, jnp.concatenate([high, low, high], axis=0), preferred_element_type=F32
    )
    slope = [x[t + 1] - x[t] for t in range(tiles + 1)]
    for t in range(tiles):
        new = mix(t) * (slope[t + 1] - slope[t]) + change[:, t * LANES : (t + 1) * LANES]
        dst[:, at + t] = jnp.where(live(t), new, x[t + 1]).reshape(levels // 8, 8, LANES)


def end_substep(src, dst, force, mix, sub, j, left_b):
    levels = left_b.shape[0]
    lane = lax.broadcasted_iota(jnp.int32, (levels, LANES), 1)
    x = [src[:, t].reshape(levels, LANES) for t in range(ENDS)]
    inner = slice(LANES, (ENDS - 1) * LANES)
    high, low = high_low(
        jnp.concatenate([jnp.concatenate(x[1:-1], axis=1), force[:, inner]], axis=0)
    )
    change = jnp.dot(
        left_b, jnp.concatenate([high, low, high], axis=0), preferred_element_type=F32
    )
    up = [pltpu.roll(v, 1, axis=1) for v in x[:-1]]
    down = [None] + [pltpu.roll(v, LANES - 1, axis=1) for v in x[1:]]
    for t in range(1, ENDS - 1):
        here = slice(t * LANES, (t + 1) * LANES)
        prior = jnp.where(lane == 0, up[t - 1], up[t])
        after = jnp.where(lane == LANES - 1, down[t + 1], down[t])
        lap = (prior - x[t]) + (after - x[t])
        new = mix[:, here] * lap + change[:, (t - 1) * LANES : t * LANES]
        dst[:, t] = jnp.where(sub[:, here] > j, new, x[t]).reshape(levels // 8, 8, LANES)


def interval_kernel(
    comps,
    doms,
    links,
    state,
    forcing,
    vertical,
    inject,
    extract,
    diffuse,
    substeps,
    landmask,
    weights,
    field_0,
    arrived,
    targets,
    end_out,
    natural,
    field_1,
    end_0,
    end_1,
    end_force,
    end_mix,
    end_sub,
    links_s,
    force_n,
    force_v,
    mix_n,
    mix_v,
    sub_n,
    sub_v,
    wet_v,
    vertical_v,
    inject_v,
    extract_v,
    weights_v,
    split_w,
    left_f,
    pick_f,
    msg,
    tgt,
    edge,
    halo,
    load_sem,
    small_sem,
    msg_send,
    msg_recv,
    tgt_send,
    tgt_recv,
    halo_send,
    halo_recv,
):
    groups, tiles = state.shape[:2]
    levels = vertical.shape[1]
    comp = lax.axis_index("comp")
    dom = lax.axis_index("dom")
    me = comp * doms + dom
    air = (comps - 1) * doms
    is_air = comp < comps - 1
    count = jnp.where(is_air, doms, air)
    first = jnp.where(is_air, air, 0)
    right = lax.rem(dom + 1, doms)
    left = lax.rem(dom + doms - 1, doms)
    runs = tiles // STEP

    small = [
        pltpu.make_async_copy(src, dst, small_sem.at[k])
        for k, (src, dst) in enumerate(
            (
                (vertical.at[0], vertical_v),
                (inject.at[0], inject_v),
                (diffuse, mix_n),
                (substeps, sub_n),
                (landmask, wet_v),
                (forcing, force_n),
                (extract.at[0], extract_v),
                (weights, weights_v),
                (links, links_s),
            )
        )
    ]
    def load(g):
        return pltpu.make_async_copy(state.at[g], natural.at[g], load_sem.at[g])

    for copy in small[:6]:
        copy.start()
    for g in range(groups):
        load(g).start()
    for copy in small[6:]:
        copy.start()

    barrier = pltpu.get_barrier_semaphore()
    for side in (left, right):
        pl.semaphore_signal(barrier, inc=1, device_id=(comp, side), device_id_type=MESH)

    def greet(p, carry):
        peer = first + p
        pl.semaphore_signal(
            barrier, inc=1, device_id=(peer // doms, peer % doms), device_id_type=MESH
        )
        return carry

    lax.fori_loop(0, count, greet, 0)

    blank_tile = jnp.zeros((groups, 8, LANES), F32)
    for field in (end_0, end_1):
        field[:, 0] = blank_tile
        field[:, ENDS - 1] = blank_tile
    for copy in small[:6]:
        copy.wait()
    mix_v[...] = jnp.transpose(mix_n[...])
    sub_v[...] = jnp.transpose(sub_n[...].astype(F32))
    for t in range(tiles):
        force_n[t] = force_n[t] * wet_v[t].astype(F32)
    for u in range(8):
        flip(force_v, u, force_n, u, tiles)
    eye = (
        lax.broadcasted_iota(jnp.int32, (levels, levels), 0)
        == lax.broadcasted_iota(jnp.int32, (levels, levels), 1)
    ).astype(F32)
    left_b = stack_left(
        left_f,
        (
            (0, vertical_v[...] * DT + eye),
            (levels, jnp.transpose(inject_v[...])[0:levels] * DT),
        ),
    )
    sides = [
        pltpu.make_async_remote_copy(
            src_ref=edge.at[k],
            dst_ref=halo.at[k],
            send_sem=halo_send.at[k],
            recv_sem=halo_recv.at[k],
            device_id=(comp, side),
            device_id_type=MESH,
        )
        for k, side in enumerate((right, left))
    ]

    def send_sides():
        for k, at in enumerate((tiles - 1, 0)):
            row = slice(at, at + 1)
            edge[k, 0:levels] = natural[:, at].reshape(levels, LANES)
            edge[k, levels : levels + 8] = force_n[at]
            edge[k, levels + 8 : levels + 16] = jnp.broadcast_to(mix_n[row], (8, LANES))
            edge[k, levels + 16 : levels + 24] = jnp.broadcast_to(
                sub_n[row].astype(F32), (8, LANES)
            )
        for copy in sides:
            copy.start()

    def take_sides():
        for copy in sides:
            copy.wait()
        for at, part in ((1, halo.at[0]), (2, edge.at[1]), (3, edge.at[0]), (4, halo.at[1])):
            there = slice(at * LANES, (at + 1) * LANES)
            end_0[:, at] = part[0:levels].reshape(levels // 8, 8, LANES)
            end_force[:, there] = part[levels : levels + 8]
            end_mix[:, there] = part[levels + 8 : levels + 9]
            end_sub[:, there] = part[levels + 16 : levels + 17].astype(jnp.int32)

    def split(s, carry):
        high, low = high_low(weights_v[s])
        split_w[s, 0:LANES] = high
        split_w[s, LANES:WIDE] = low
        return carry

    def send(p):
        peer = first + p
        spot = (peer // doms, peer % doms)
        return (
            pltpu.make_async_remote_copy(
                src_ref=msg.at[p],
                dst_ref=arrived.at[me],
                send_sem=msg_send.at[p],
                recv_sem=msg_recv.at[me],
                device_id=spot,
                device_id_type=MESH,
            ),
            pltpu.make_async_remote_copy(
                src_ref=tgt.at[p],
                dst_ref=targets.at[me],
                send_sem=tgt_send.at[p],
                recv_sem=tgt_recv.at[me],
                device_id=spot,
                device_id_type=MESH,
            ),
        )

    lane = lax.broadcasted_iota(jnp.int32, (1, LANES), 1)
    blank = jnp.zeros((PAD_ROWS - levels, LANES), F32)

    def group(step, pick_b):
        rows = []
        for q in range(GROUP):
            peer = first + step * GROUP + q
            for k in range(2):
                block = jnp.maximum(links_s[0, 0, k, peer], 0)
                x = natural[:, block].reshape(levels, LANES)
                wet = wet_v[block]
                high, low = high_low(jnp.concatenate([x, blank], axis=0))
                rows.append((jnp.concatenate([high, low, high], axis=0), wet))
        outs = []
        for m in range(0, 2 * GROUP, 2):
            both = jnp.dot(
                pick_b,
                jnp.concatenate([rows[m][0], rows[m + 1][0]], axis=1),
                preferred_element_type=F32,
            )
            for k in range(2):
                r = both[:, k * LANES : (k + 1) * LANES] * rows[m + k][1].astype(F32)
                high = r.astype(BF16).astype(F32)
                low = r - high
                top = jnp.concatenate([high, high], axis=1)
                bottom = jnp.concatenate([low, jnp.zeros_like(low)], axis=1)
                lhs = jnp.concatenate([top, bottom], axis=0).astype(BF16)
                slot = jnp.maximum(links_s[2, 0, k, first + step * GROUP + m // 2], 0)
                out = jnp.dot(lhs, split_w[slot], preferred_element_type=F32)
                outs.append(out[0:8] + out[8:16])
        for q in range(GROUP):
            p = step * GROUP + q
            peer = first + p
            msg[p] = jnp.concatenate(outs[2 * q : 2 * q + 2], axis=0)
            t0 = jnp.where(lane == 0, links_s[1, 0, 0, peer], -1)
            tgt[p] = jnp.where(lane == 1, links_s[1, 0, 1, peer], t0)
        for q in range(GROUP):
            for copy in send(step * GROUP + q):
                copy.start()
        return pick_b

    def send_all():
        for copy in small[6:]:
            copy.wait()
        pl.semaphore_wait(barrier, count + 2)
        send_sides()
        pick_b = stack_left(pick_f, ((0, extract_v[...]),))
        lax.fori_loop(0, weights_v.shape[0], split, 0, unroll=4)
        lax.fori_loop(0, count // GROUP, group, pick_b)

    def enter(g, carry):
        load(g).wait()
        for u in range(8):
            flip(field_0, (g * (tiles + 2) + 1) * 8 + u, natural, g * tiles * 8 + u, tiles)
        return carry

    lax.fori_loop(0, groups, enter, 0)

    def run(src, dst, j):
        last = src[:, tiles].reshape(levels, LANES)
        src[:, 0] = pltpu.roll(last, 1, axis=1).reshape(groups, 8, LANES)
        following = src[:, 1].reshape(levels, LANES)
        src[:, tiles + 1] = pltpu.roll(following, LANES - 1, axis=1).reshape(groups, 8, LANES)
        stage = j.astype(F32)

        def part(i, carry):
            at = i * STEP
            substep(
                src,
                dst,
                1 + at,
                STEP,
                lambda t: force_v[at + t],
                lambda t: mix_v[pl.ds(at + t, 1), :],
                lambda t: sub_v[pl.ds(at + t, 1), :] > stage,
                left_b,
            )
            return carry

        lax.fori_loop(0, runs, part, 0)

    def twice(pair, carry):
        run(field_0, field_1, 2 * pair)

        @pl.when(pair == 0)
        def _():
            send_all()

        run(field_1, field_0, 2 * pair + 1)
        return carry

    lax.fori_loop(0, SUBS // 2, twice, 0)
    take_sides()

    def end_twice(pair, carry):
        end_substep(end_0, end_1, end_force, end_mix, end_sub, 2 * pair, left_b)
        end_substep(end_1, end_0, end_force, end_mix, end_sub, 2 * pair + 1, left_b)
        return carry

    lax.fori_loop(0, SUBS // 2, end_twice, 0)
    end_out[:, 0] = end_0[:, 2]
    end_out[:, 1] = end_0[:, 3]

    def finish(p, carry):
        for copy in send(p):
            copy.wait_send()
        g = first + p
        pltpu.make_async_copy(arrived.at[g], arrived.at[g], msg_recv.at[g]).wait()
        pltpu.make_async_copy(targets.at[g], targets.at[g], tgt_recv.at[g]).wait()
        return carry

    lax.fori_loop(0, count, finish, 0)


def interval(comps, doms, links, state, forcing, vertical, inject, extract, diffuse, substeps, landmask, weights):
    groups, tiles = state.shape[:2]
    levels, fields = vertical.shape[1], forcing.shape[1]
    slots = weights.shape[0]
    devices = comps * doms
    peers = max(doms, devices - doms)
    stack = (groups, tiles + 2, 8, LANES)
    ends = (groups, ENDS, 8, LANES)
    square = (tiles, LANES)
    hbm = pl.BlockSpec(memory_space=pltpu.HBM)
    vmem = pl.BlockSpec(memory_space=pltpu.VMEM)
    edge_rows = levels + 24
    return pl.pallas_call(
        functools.partial(interval_kernel, comps, doms),
        out_shape=(
            pltpu.VMEM(stack, F32),
            jax.ShapeDtypeStruct((devices, 2 * fields, LANES), F32),
            jax.ShapeDtypeStruct((devices, 1, LANES), jnp.int32),
            pltpu.VMEM((groups, 2, 8, LANES), F32),
        ),
        in_specs=[hbm] * 10,
        out_specs=(vmem, hbm, hbm, vmem),
        scratch_shapes=[
            pltpu.VMEM(state.shape, F32),
            pltpu.VMEM(stack, F32),
            pltpu.VMEM(ends, F32),
            pltpu.VMEM(ends, F32),
            pltpu.VMEM((fields, ENDS * LANES), F32),
            pltpu.VMEM((1, ENDS * LANES), F32),
            pltpu.VMEM((1, ENDS * LANES), jnp.int32),
            pltpu.SMEM(links.shape, jnp.int32),
            pltpu.VMEM(forcing.shape, F32),
            pltpu.VMEM(forcing.shape, F32),
            pltpu.VMEM(square, F32),
            pltpu.VMEM(square, F32),
            pltpu.VMEM(square, jnp.int32),
            pltpu.VMEM(square, F32),
            pltpu.VMEM((tiles, 1, LANES), jnp.int32),
            pltpu.VMEM((levels, levels), F32),
            pltpu.VMEM((fields, levels), F32),
            pltpu.VMEM((fields, levels), F32),
            pltpu.VMEM(weights.shape, F32),
            pltpu.VMEM((slots, WIDE, LANES), BF16),
            pltpu.VMEM((levels, WIDE), F32),
            pltpu.VMEM((fields, WIDE), F32),
            pltpu.VMEM((peers, 2 * fields, LANES), F32),
            pltpu.VMEM((peers, 1, LANES), jnp.int32),
            pltpu.VMEM((2, edge_rows, LANES), F32),
            pltpu.VMEM((2, edge_rows, LANES), F32),
            pltpu.SemaphoreType.DMA((groups,)),
            pltpu.SemaphoreType.DMA((9,)),
            pltpu.SemaphoreType.DMA((peers,)),
            pltpu.SemaphoreType.DMA((devices,)),
            pltpu.SemaphoreType.DMA((peers,)),
            pltpu.SemaphoreType.DMA((devices,)),
            pltpu.SemaphoreType.DMA((2,)),
            pltpu.SemaphoreType.DMA((2,)),
        ],
        compiler_params=pltpu.CompilerParams(
            collective_id=0, has_side_effects=True, vmem_limit_bytes=40 << 20
        ),
        name="interval",
    )(
        *(
            pltpu.with_memory_space_constraint(a, pltpu.HBM)
            for a in (
                links, state, forcing, vertical, inject, extract, diffuse, substeps, landmask, weights
            )
        )
    )


def deliver_kernel(
    comps, doms, targets, arrived, result, ends, state_next, forcing_next, targets_s, arrived_v, next_v, natural, sems
):
    groups, tiles = state_next.shape[:2]
    get_targets = pltpu.make_async_copy(targets, targets_s, sems.at[0])
    get_arrived = pltpu.make_async_copy(arrived, arrived_v, sems.at[1])
    get_targets.start()
    get_arrived.start()

    def store(g):
        return pltpu.make_async_copy(natural.at[g], state_next.at[g], sems.at[3 + g])

    near = lax.broadcasted_iota(jnp.int32, (8, LANES), 1) < LANES // 2

    def leave(g, carry):
        for u in range(8):
            flip(natural, g * tiles * 8 + u, result, (g * (tiles + 2) + 1) * 8 + u, tiles)
        natural[g, 0] = jnp.where(near, ends[g, 0], natural[g, 0])
        natural[g, tiles - 1] = jnp.where(near, natural[g, tiles - 1], ends[g, 1])
        store(g).start()
        return carry

    lax.fori_loop(0, groups, leave, 0)
    next_v[...] = jnp.zeros_like(next_v)
    air = (comps - 1) * doms
    is_air = lax.axis_index("comp") < comps - 1
    count = jnp.where(is_air, doms, air)
    first = jnp.where(is_air, air, 0)
    get_targets.wait()
    get_arrived.wait()

    def scatter(p, carry):
        for k in range(2):
            t = targets_s[first + p, 0, k]
            there = pl.ds(pl.multiple_of(jnp.maximum(t, 0) * LANES, LANES), LANES)
            part = arrived_v[first + p, k * 8 : (k + 1) * 8]
            next_v[:, there] += jnp.where(t >= 0, part, jnp.zeros_like(part))
        return carry

    lax.fori_loop(0, count, scatter, 0)
    store_next = pltpu.make_async_copy(next_v, forcing_next, sems.at[2])
    store_next.start()
    for g in range(groups):
        store(g).wait()
    store_next.wait()


def deliver(comps, doms, targets, arrived, result, ends, fields):
    hbm = pl.BlockSpec(memory_space=pltpu.HBM)
    vmem = pl.BlockSpec(memory_space=pltpu.VMEM)
    groups, tiles = result.shape[0], result.shape[1] - 2
    columns = tiles * LANES
    return pl.pallas_call(
        functools.partial(deliver_kernel, comps, doms),
        out_shape=(
            jax.ShapeDtypeStruct((groups, tiles, 8, LANES), F32),
            jax.ShapeDtypeStruct((fields, columns), F32),
        ),
        in_specs=[hbm, hbm, vmem, vmem],
        out_specs=(hbm, hbm),
        scratch_shapes=[
            pltpu.SMEM(targets.shape, jnp.int32),
            pltpu.VMEM(arrived.shape, F32),
            pltpu.VMEM((fields, columns), F32),
            pltpu.VMEM((groups, tiles, 8, LANES), F32),
            pltpu.SemaphoreType.DMA((3 + groups,)),
        ],
        compiler_params=pltpu.CompilerParams(vmem_limit_bytes=12 << 20),
        name="deliver",
    )(targets, arrived, *(pltpu.with_memory_space_constraint(a, pltpu.VMEM) for a in (result, ends)))


def solution(mesh):
    comps, doms = mesh.shape["comp"], mesh.shape["dom"]

    def local(state, forcing, vertical, inject, extract, diffuse, substeps, landmask, links, weights):
        levels, columns = state.shape
        tiles = state.reshape(levels // 8, 8, columns // LANES, LANES).swapaxes(1, 2)
        result, arrived, targets, ends = interval(
            comps,
            doms,
            links.swapaxes(2, 3),
            tiles,
            forcing.reshape(-1, columns // LANES, LANES).swapaxes(0, 1),
            vertical,
            inject.swapaxes(1, 2),
            extract,
            diffuse.reshape(-1, LANES),
            substeps.reshape(-1, LANES),
            landmask.reshape(-1, 1, LANES),
            weights,
        )
        new, forcing_next = deliver(comps, doms, targets, arrived, result, ends, forcing.shape[0])
        return new.swapaxes(1, 2).reshape(state.shape), forcing_next

    return jax.shard_map(
        local,
        mesh=mesh,
        in_specs=(
            P(None, ("comp", "dom")),
            P(None, ("comp", "dom")),
            P("comp", None, None),
            P("comp", None, None),
            P("comp", None, None),
            P(("comp", "dom")),
            P(("comp", "dom")),
            P(("comp", "dom")),
            P(None, ("comp", "dom"), None, None),
            P(("comp", "dom"), None, None),
        ),
        out_specs=(P(None, ("comp", "dom")), P(None, ("comp", "dom"))),
        check_vma=False,
    )
```

```python
import functools
import math

import jax
import jax.numpy as jnp
from jax import lax
from jax.experimental import pallas as pl
from jax.experimental.pallas import tpu as pltpu
from jax.sharding import PartitionSpec as P

SUBS = 4
DT = 0.25
LANES = 128
WIDE = 256
STEP = 64
BATCH = 3
ENDS = 6
GROUP = 8
PAD_ROWS = 80
MESH = pl.DeviceIdType.MESH
F32 = jnp.float32
BF16 = jnp.bfloat16


def high_low(x):
    high = x.astype(BF16)
    return high, (x - high.astype(F32)).astype(BF16)


def stack_left(scratch, parts):
    scratch[...] = jnp.zeros_like(scratch)
    for at, matrix in parts:
        high = matrix.astype(BF16).astype(F32)
        size = matrix.shape[1]
        for k, value in enumerate((high, high, matrix - high)):
            scratch[:, k * PAD_ROWS + at : k * PAD_ROWS + at + size] = value
    return scratch[...].astype(BF16)[:, : 3 * PAD_ROWS]


def flip(dst, to, src, at, tiles):
    flat = [ref.reshape(math.prod(ref.shape[:-1]), LANES) for ref in (dst, src)]
    value = flat[1][pl.ds(at, tiles, stride=8), :]
    flat[0][pl.ds(to, tiles, stride=8), :] = jnp.transpose(value)


def substep(src, dst, at, tiles, force, mix, live, left_b):
    levels = left_b.shape[0]
    x = [src[:, at + t].reshape(levels, LANES) for t in range(-1, tiles + 1)]
    values = jnp.concatenate(x[1:-1], axis=1)
    high, low = high_low(
        jnp.concatenate([values, jnp.concatenate([force(t) for t in range(tiles)], axis=1)], axis=0)
    )
    change = jnp.dot(
        left_b, jnp.concatenate([high, low, high], axis=0), preferred_element_type=F32
    )
    slope = [x[t + 1] - x[t] for t in range(tiles + 1)]
    for t in range(tiles):
        new = mix(t) * (slope[t + 1] - slope[t]) + change[:, t * LANES : (t + 1) * LANES]
        dst[:, at + t] = jnp.where(live(t), new, x[t + 1]).reshape(levels // 8, 8, LANES)


def end_substep(src, dst, force, mix, sub, j, left_b):
    levels = left_b.shape[0]
    lane = lax.broadcasted_iota(jnp.int32, (levels, LANES), 1)
    x = [src[:, t].reshape(levels, LANES) for t in range(ENDS)]
    inner = slice(LANES, (ENDS - 1) * LANES)
    high, low = high_low(
        jnp.concatenate([jnp.concatenate(x[1:-1], axis=1), force[:, inner]], axis=0)
    )
    change = jnp.dot(
        left_b, jnp.concatenate([high, low, high], axis=0), preferred_element_type=F32
    )
    up = [pltpu.roll(v, 1, axis=1) for v in x[:-1]]
    down = [None] + [pltpu.roll(v, LANES - 1, axis=1) for v in x[1:]]
    for t in range(1, ENDS - 1):
        here = slice(t * LANES, (t + 1) * LANES)
        prior = jnp.where(lane == 0, up[t - 1], up[t])
        after = jnp.where(lane == LANES - 1, down[t + 1], down[t])
        lap = (prior - x[t]) + (after - x[t])
        new = mix[:, here] * lap + change[:, (t - 1) * LANES : t * LANES]
        dst[:, t] = jnp.where(sub[:, here] > j, new, x[t]).reshape(levels // 8, 8, LANES)


def interval_kernel(
    comps,
    doms,
    links,
    state,
    forcing,
    vertical,
    inject,
    extract,
    diffuse,
    substeps,
    landmask,
    weights,
    field_0,
    arrived,
    targets,
    end_out,
    natural,
    field_1,
    end_0,
    end_1,
    end_force,
    end_mix,
    end_sub,
    links_s,
    force_n,
    force_v,
    mix_n,
    mix_v,
    sub_n,
    sub_v,
    wet_v,
    vertical_v,
    inject_v,
    extract_v,
    weights_v,
    split_w,
    left_f,
    pick_f,
    msg,
    edge,
    halo,
    load_sem,
    small_sem,
    msg_send,
    msg_recv,
    halo_send,
    halo_recv,
):
    groups, tiles = state.shape[:2]
    levels = vertical.shape[1]
    comp = lax.axis_index("comp")
    dom = lax.axis_index("dom")
    me = comp * doms + dom
    air = (comps - 1) * doms
    is_air = comp < comps - 1
    count = jnp.where(is_air, doms, air)
    first = jnp.where(is_air, air, 0)
    right = lax.rem(dom + 1, doms)
    left = lax.rem(dom + doms - 1, doms)
    runs = tiles // STEP

    small = [
        pltpu.make_async_copy(src, dst, small_sem.at[k])
        for k, (src, dst) in enumerate(
            (
                (vertical.at[0], vertical_v),
                (inject.at[0], inject_v),
                (diffuse, mix_n),
                (substeps, sub_n),
                (landmask, wet_v),
                (forcing, force_n),
                (extract.at[0], extract_v),
                (weights, weights_v),
                (links, links_s),
            )
        )
    ]
    def load(g):
        return pltpu.make_async_copy(state.at[g], natural.at[g], load_sem.at[g])

    for copy in small[:6]:
        copy.start()
    for g in range(groups):
        load(g).start()
    for copy in small[6:]:
        copy.start()

    barrier = pltpu.get_barrier_semaphore()
    for side in (left, right):
        pl.semaphore_signal(barrier, inc=1, device_id=(comp, side), device_id_type=MESH)

    def greet(p, carry):
        peer = first + p
        pl.semaphore_signal(
            barrier, inc=1, device_id=(peer // doms, peer % doms), device_id_type=MESH
        )
        return carry

    lax.fori_loop(0, count, greet, 0)

    blank_tile = jnp.zeros((groups, 8, LANES), F32)
    for field in (end_0, end_1):
        field[:, 0] = blank_tile
        field[:, ENDS - 1] = blank_tile
    for copy in small[:6]:
        copy.wait()
    mix_v[...] = jnp.transpose(mix_n[...])
    sub_v[...] = jnp.transpose(sub_n[...].astype(F32))
    for t in range(tiles):
        force_n[t] = force_n[t] * wet_v[t].astype(F32)
    for u in range(8):
        flip(force_v, u, force_n, u, tiles)
    eye = (
        lax.broadcasted_iota(jnp.int32, (levels, levels), 0)
        == lax.broadcasted_iota(jnp.int32, (levels, levels), 1)
    ).astype(F32)
    left_b = stack_left(
        left_f,
        (
            (0, vertical_v[...] * DT + eye),
            (levels, jnp.transpose(inject_v[...])[0:levels] * DT),
        ),
    )
    sides = [
        pltpu.make_async_remote_copy(
            src_ref=edge.at[k],
            dst_ref=halo.at[k],
            send_sem=halo_send.at[k],
            recv_sem=halo_recv.at[k],
            device_id=(comp, side),
            device_id_type=MESH,
        )
        for k, side in enumerate((right, left))
    ]

    def send_sides():
        for k, at in enumerate((tiles - 1, 0)):
            row = slice(at, at + 1)
            edge[k, 0:levels] = natural[:, at].reshape(levels, LANES)
            edge[k, levels : levels + 8] = force_n[at]
            edge[k, levels + 8 : levels + 16] = jnp.broadcast_to(mix_n[row], (8, LANES))
            edge[k, levels + 16 : levels + 24] = jnp.broadcast_to(
                sub_n[row].astype(F32), (8, LANES)
            )
        for copy in sides:
            copy.start()

    def take_sides():
        for copy in sides:
            copy.wait()
        for at, part in ((1, halo.at[0]), (2, edge.at[1]), (3, edge.at[0]), (4, halo.at[1])):
            there = slice(at * LANES, (at + 1) * LANES)
            end_0[:, at] = part[0:levels].reshape(levels // 8, 8, LANES)
            end_force[:, there] = part[levels : levels + 8]
            end_mix[:, there] = part[levels + 8 : levels + 9]
            end_sub[:, there] = part[levels + 16 : levels + 17].astype(jnp.int32)

    def split(s, carry):
        high, low = high_low(weights_v[s])
        split_w[s, 0:LANES] = high
        split_w[s, LANES:WIDE] = low
        return carry

    def send(p):
        peer = first + p
        return pltpu.make_async_remote_copy(
            src_ref=msg.at[p],
            dst_ref=arrived.at[me],
            send_sem=msg_send.at[p],
            recv_sem=msg_recv.at[me],
            device_id=(peer // doms, peer % doms),
            device_id_type=MESH,
        )

    lane = lax.broadcasted_iota(jnp.int32, (8, LANES), 1)
    blank = jnp.zeros((PAD_ROWS - levels, LANES), F32)

    def form(step, pick_b):
        rows = []
        for q in range(GROUP):
            peer = first + step * GROUP + q
            for k in range(2):
                block = jnp.maximum(links_s[0, 0, k, peer], 0)
                x = natural[:, block].reshape(levels, LANES)
                wet = wet_v[block]
                high, low = high_low(jnp.concatenate([x, blank], axis=0))
                rows.append((jnp.concatenate([high, low, high], axis=0), wet))
        outs = []
        for m in range(0, 2 * GROUP, 2):
            both = jnp.dot(
                pick_b,
                jnp.concatenate([rows[m][0], rows[m + 1][0]], axis=1),
                preferred_element_type=F32,
            )
            for k in range(2):
                r = both[:, k * LANES : (k + 1) * LANES] * rows[m + k][1].astype(F32)
                high = r.astype(BF16).astype(F32)
                low = r - high
                top = jnp.concatenate([high, high], axis=1)
                bottom = jnp.concatenate([low, jnp.zeros_like(low)], axis=1)
                lhs = jnp.concatenate([top, bottom], axis=0).astype(BF16)
                slot = jnp.maximum(links_s[2, 0, k, first + step * GROUP + m // 2], 0)
                out = jnp.dot(lhs, split_w[slot], preferred_element_type=F32)
                outs.append(out[0:8] + out[8:16])
        for q in range(GROUP):
            p = step * GROUP + q
            peer = first + p
            t0 = jnp.where(lane == 0, links_s[1, 0, 0, peer].astype(F32), -1.0)
            t1 = jnp.where(lane == 1, links_s[1, 0, 1, peer].astype(F32), t0)
            msg[p] = jnp.concatenate(outs[2 * q : 2 * q + 2] + [t1], axis=0)

    def start(step):
        for q in range(GROUP):
            send(step * GROUP + q).start()

    def form_next(step, pick_b):
        start(step - 1)
        form(step, pick_b)
        return pick_b

    def send_all():
        for copy in small[6:]:
            copy.wait()
        pl.semaphore_wait(barrier, count + 2)
        send_sides()
        pick_b = stack_left(pick_f, ((0, extract_v[...]),))
        lax.fori_loop(0, weights_v.shape[0], split, 0, unroll=4)
        form(0, pick_b)
        lax.fori_loop(1, count // GROUP, form_next, pick_b)
        start(count // GROUP - 1)

    def enter(step, carry):
        for v in range(BATCH):
            load(step * BATCH + v).wait()
        for v in range(BATCH):
            g = step * BATCH + v
            for u in range(8):
                flip(field_0, (g * (tiles + 2) + 1) * 8 + u, natural, g * tiles * 8 + u, tiles)
        return carry

    lax.fori_loop(0, groups // BATCH, enter, 0)

    def run(src, dst, j, early):
        last = src[:, tiles].reshape(levels, LANES)
        src[:, 0] = pltpu.roll(last, 1, axis=1).reshape(groups, 8, LANES)
        following = src[:, 1].reshape(levels, LANES)
        src[:, tiles + 1] = pltpu.roll(following, LANES - 1, axis=1).reshape(groups, 8, LANES)
        stage = j.astype(F32)

        def part(i, carry):
            at = i * STEP
            if early:

                @pl.when((j == 0) & (i == 1))
                def _():
                    send_all()

            substep(
                src,
                dst,
                1 + at,
                STEP,
                lambda t: force_v[at + t],
                lambda t: mix_v[pl.ds(at + t, 1), :],
                lambda t: sub_v[pl.ds(at + t, 1), :] > stage,
                left_b,
            )
            return carry

        lax.fori_loop(0, runs, part, 0)

    def twice(pair, carry):
        run(field_0, field_1, 2 * pair, True)

        run(field_1, field_0, 2 * pair + 1, False)
        return carry

    lax.fori_loop(0, SUBS // 2, twice, 0)
    take_sides()

    def end_twice(pair, carry):
        end_substep(end_0, end_1, end_force, end_mix, end_sub, 2 * pair, left_b)
        end_substep(end_1, end_0, end_force, end_mix, end_sub, 2 * pair + 1, left_b)
        return carry

    lax.fori_loop(0, SUBS // 2, end_twice, 0)
    end_out[:, 0] = end_0[:, 2]
    end_out[:, 1] = end_0[:, 3]

    def finish(p, carry):
        send(p).wait_send()
        g = first + p
        pltpu.make_async_copy(arrived.at[g], arrived.at[g], msg_recv.at[g]).wait()
        return carry

    lax.fori_loop(0, count, finish, 0)
    fields = inject.shape[1]
    targets[...] = arrived[:, 2 * fields, :].astype(jnp.int32)


def interval(comps, doms, links, state, forcing, vertical, inject, extract, diffuse, substeps, landmask, weights):
    groups, tiles = state.shape[:2]
    levels, fields = vertical.shape[1], forcing.shape[1]
    slots = weights.shape[0]
    devices = comps * doms
    peers = max(doms, devices - doms)
    stack = (groups, tiles + 2, 8, LANES)
    ends = (groups, ENDS, 8, LANES)
    square = (tiles, LANES)
    hbm = pl.BlockSpec(memory_space=pltpu.HBM)
    vmem = pl.BlockSpec(memory_space=pltpu.VMEM)
    edge_rows = levels + 24
    return pl.pallas_call(
        functools.partial(interval_kernel, comps, doms),
        out_shape=(
            pltpu.VMEM(stack, F32),
            pltpu.VMEM((devices, 2 * fields + 8, LANES), F32),
            pltpu.VMEM((devices, LANES), jnp.int32),
            pltpu.VMEM((groups, 2, 8, LANES), F32),
        ),
        in_specs=[hbm] * 10,
        out_specs=(vmem, vmem, vmem, vmem),
        scratch_shapes=[
            pltpu.VMEM(state.shape, F32),
            pltpu.VMEM(stack, F32),
            pltpu.VMEM(ends, F32),
            pltpu.VMEM(ends, F32),
            pltpu.VMEM((fields, ENDS * LANES), F32),
            pltpu.VMEM((1, ENDS * LANES), F32),
            pltpu.VMEM((1, ENDS * LANES), jnp.int32),
            pltpu.SMEM(links.shape, jnp.int32),
            pltpu.VMEM(forcing.shape, F32),
            pltpu.VMEM(forcing.shape, F32),
            pltpu.VMEM(square, F32),
            pltpu.VMEM(square, F32),
            pltpu.VMEM(square, jnp.int32),
            pltpu.VMEM(square, F32),
            pltpu.VMEM((tiles, 1, LANES), jnp.int32),
            pltpu.VMEM((levels, levels), F32),
            pltpu.VMEM((fields, levels), F32),
            pltpu.VMEM((fields, levels), F32),
            pltpu.VMEM(weights.shape, F32),
            pltpu.VMEM((slots, WIDE, LANES), BF16),
            pltpu.VMEM((levels, WIDE), F32),
            pltpu.VMEM((fields, WIDE), F32),
            pltpu.VMEM((peers, 2 * fields + 8, LANES), F32),
            pltpu.VMEM((2, edge_rows, LANES), F32),
            pltpu.VMEM((2, edge_rows, LANES), F32),
            pltpu.SemaphoreType.DMA((groups,)),
            pltpu.SemaphoreType.DMA((9,)),
            pltpu.SemaphoreType.DMA((peers,)),
            pltpu.SemaphoreType.DMA((devices,)),
            pltpu.SemaphoreType.DMA((2,)),
            pltpu.SemaphoreType.DMA((2,)),
        ],
        compiler_params=pltpu.CompilerParams(
            collective_id=0, has_side_effects=True, vmem_limit_bytes=40 << 20
        ),
        name="interval",
    )(
        *(
            pltpu.with_memory_space_constraint(a, pltpu.HBM)
            for a in (
                links, state, forcing, vertical, inject, extract, diffuse, substeps, landmask, weights
            )
        )
    )


def deliver_kernel(
    comps, doms, targets, arrived, result, ends, state_next, forcing_next, targets_s, next_v, natural, sems
):
    groups, tiles = state_next.shape[:2]
    get_targets = pltpu.make_async_copy(targets, targets_s, sems.at[0])
    get_targets.start()

    def store(g):
        return pltpu.make_async_copy(natural.at[g], state_next.at[g], sems.at[3 + g])

    near = lax.broadcasted_iota(jnp.int32, (8, LANES), 1) < LANES // 2

    def leave(step, carry):
        for v in range(BATCH):
            g = step * BATCH + v
            for u in range(8):
                flip(natural, g * tiles * 8 + u, result, (g * (tiles + 2) + 1) * 8 + u, tiles)
        for v in range(BATCH):
            g = step * BATCH + v
            natural[g, 0] = jnp.where(near, ends[g, 0], natural[g, 0])
            natural[g, tiles - 1] = jnp.where(near, natural[g, tiles - 1], ends[g, 1])
            store(g).start()
        return carry

    lax.fori_loop(0, groups // BATCH, leave, 0)
    next_v[...] = jnp.zeros_like(next_v)
    air = (comps - 1) * doms
    is_air = lax.axis_index("comp") < comps - 1
    count = jnp.where(is_air, doms, air)
    first = jnp.where(is_air, air, 0)
    get_targets.wait()

    def scatter(p, carry):
        for k in range(2):
            t = targets_s[first + p, k]
            there = pl.ds(pl.multiple_of(jnp.maximum(t, 0) * LANES, LANES), LANES)
            part = arrived[first + p, k * 8 : (k + 1) * 8]
            next_v[:, there] += jnp.where(t >= 0, part, jnp.zeros_like(part))
        return carry

    lax.fori_loop(0, count, scatter, 0)
    store_next = pltpu.make_async_copy(next_v, forcing_next, sems.at[2])
    store_next.start()
    for g in range(groups):
        store(g).wait()
    store_next.wait()


def deliver(comps, doms, targets, arrived, result, ends, fields):
    hbm = pl.BlockSpec(memory_space=pltpu.HBM)
    vmem = pl.BlockSpec(memory_space=pltpu.VMEM)
    groups, tiles = result.shape[0], result.shape[1] - 2
    columns = tiles * LANES
    return pl.pallas_call(
        functools.partial(deliver_kernel, comps, doms),
        out_shape=(
            jax.ShapeDtypeStruct((groups, tiles, 8, LANES), F32),
            jax.ShapeDtypeStruct((fields, columns), F32),
        ),
        in_specs=[vmem] * 4,
        out_specs=(hbm, hbm),
        scratch_shapes=[
            pltpu.SMEM(targets.shape, jnp.int32),
            pltpu.VMEM((fields, columns), F32),
            pltpu.VMEM((groups, tiles, 8, LANES), F32),
            pltpu.SemaphoreType.DMA((3 + groups,)),
        ],
        compiler_params=pltpu.CompilerParams(vmem_limit_bytes=12 << 20),
        name="deliver",
    )(
        *(
            pltpu.with_memory_space_constraint(a, pltpu.VMEM)
            for a in (targets, arrived, result, ends)
        )
    )


def solution(mesh):
    comps, doms = mesh.shape["comp"], mesh.shape["dom"]

    def local(state, forcing, vertical, inject, extract, diffuse, substeps, landmask, links, weights):
        levels, columns = state.shape
        tiles = state.reshape(levels // 8, 8, columns // LANES, LANES).swapaxes(1, 2)
        result, arrived, targets, ends = interval(
            comps,
            doms,
            links.swapaxes(2, 3),
            tiles,
            forcing.reshape(-1, columns // LANES, LANES).swapaxes(0, 1),
            vertical,
            inject.swapaxes(1, 2),
            extract,
            diffuse.reshape(-1, LANES),
            substeps.reshape(-1, LANES),
            landmask.reshape(-1, 1, LANES),
            weights,
        )
        new, forcing_next = deliver(comps, doms, targets, arrived, result, ends, forcing.shape[0])
        return new.swapaxes(1, 2).reshape(state.shape), forcing_next

    return jax.shard_map(
        local,
        mesh=mesh,
        in_specs=(
            P(None, ("comp", "dom")),
            P(None, ("comp", "dom")),
            P("comp", None, None),
            P("comp", None, None),
            P("comp", None, None),
            P(("comp", "dom")),
            P(("comp", "dom")),
            P(("comp", "dom")),
            P(None, ("comp", "dom"), None, None),
            P(("comp", "dom"), None, None),
        ),
        out_specs=(P(None, ("comp", "dom")), P(None, ("comp", "dom"))),
        check_vma=False,
    )
```

```python
import functools
import math

import jax
import jax.numpy as jnp
from jax import lax
from jax.experimental import pallas as pl
from jax.experimental.pallas import tpu as pltpu
from jax.sharding import PartitionSpec as P

SUBS = 4
DT = 0.25
LANES = 128
WIDE = 256
STEP = 64
BATCH = 3
ENDS = 6
GROUP = 8
PAD_ROWS = 80
MESH = pl.DeviceIdType.MESH
F32 = jnp.float32
BF16 = jnp.bfloat16


def high_low(x):
    high = x.astype(BF16)
    return high, (x - high.astype(F32)).astype(BF16)


def stack_left(scratch, parts):
    scratch[...] = jnp.zeros_like(scratch)
    for at, matrix in parts:
        high = matrix.astype(BF16).astype(F32)
        size = matrix.shape[1]
        for k, value in enumerate((high, high, matrix - high)):
            scratch[:, k * PAD_ROWS + at : k * PAD_ROWS + at + size] = value
    return scratch[...].astype(BF16)[:, : 3 * PAD_ROWS]


def flip(dst, to, src, at, tiles):
    flat = [ref.reshape(math.prod(ref.shape[:-1]), LANES) for ref in (dst, src)]
    value = flat[1][pl.ds(at, tiles, stride=8), :]
    flat[0][pl.ds(to, tiles, stride=8), :] = jnp.transpose(value)


def substep(src, dst, at, tiles, force, mix, live, left_b):
    levels = left_b.shape[0]
    x = [src[:, at + t].reshape(levels, LANES) for t in range(-1, tiles + 1)]
    values = jnp.concatenate(x[1:-1], axis=1)
    high, low = high_low(
        jnp.concatenate([values, jnp.concatenate([force(t) for t in range(tiles)], axis=1)], axis=0)
    )
    change = jnp.dot(
        left_b, jnp.concatenate([high, low, high], axis=0), preferred_element_type=F32
    )
    slope = [x[t + 1] - x[t] for t in range(tiles + 1)]
    for t in range(tiles):
        new = mix(t) * (slope[t + 1] - slope[t]) + change[:, t * LANES : (t + 1) * LANES]
        dst[:, at + t] = jnp.where(live(t), new, x[t + 1]).reshape(levels // 8, 8, LANES)


def end_substep(src, dst, force, mix, sub, j, left_b):
    levels = left_b.shape[0]
    lane = lax.broadcasted_iota(jnp.int32, (levels, LANES), 1)
    x = [src[:, t].reshape(levels, LANES) for t in range(ENDS)]
    inner = slice(LANES, (ENDS - 1) * LANES)
    high, low = high_low(
        jnp.concatenate([jnp.concatenate(x[1:-1], axis=1), force[:, inner]], axis=0)
    )
    change = jnp.dot(
        left_b, jnp.concatenate([high, low, high], axis=0), preferred_element_type=F32
    )
    up = [pltpu.roll(v, 1, axis=1) for v in x[:-1]]
    down = [None] + [pltpu.roll(v, LANES - 1, axis=1) for v in x[1:]]
    for t in range(1, ENDS - 1):
        here = slice(t * LANES, (t + 1) * LANES)
        prior = jnp.where(lane == 0, up[t - 1], up[t])
        after = jnp.where(lane == LANES - 1, down[t + 1], down[t])
        lap = (prior - x[t]) + (after - x[t])
        new = mix[:, here] * lap + change[:, (t - 1) * LANES : t * LANES]
        dst[:, t] = jnp.where(sub[:, here] > j, new, x[t]).reshape(levels // 8, 8, LANES)


def interval_kernel(
    comps,
    doms,
    links,
    state,
    forcing,
    vertical,
    inject,
    extract,
    diffuse,
    substeps,
    landmask,
    weights,
    field_0,
    arrived,
    targets,
    end_out,
    natural,
    field_1,
    end_0,
    end_1,
    end_force,
    end_mix,
    end_sub,
    links_s,
    force_n,
    force_v,
    mix_n,
    mix_v,
    sub_n,
    sub_v,
    wet_v,
    vertical_v,
    inject_v,
    extract_v,
    weights_v,
    split_w,
    left_f,
    pick_f,
    msg,
    edge,
    halo,
    load_sem,
    small_sem,
    msg_send,
    msg_recv,
    halo_send,
    halo_recv,
):
    groups, tiles = state.shape[:2]
    levels = vertical.shape[1]
    comp = lax.axis_index("comp")
    dom = lax.axis_index("dom")
    me = comp * doms + dom
    air = (comps - 1) * doms
    is_air = comp < comps - 1
    count = jnp.where(is_air, doms, air)
    first = jnp.where(is_air, air, 0)
    right = lax.rem(dom + 1, doms)
    left = lax.rem(dom + doms - 1, doms)
    runs = tiles // STEP

    small = [
        pltpu.make_async_copy(src, dst, small_sem.at[k])
        for k, (src, dst) in enumerate(
            (
                (vertical.at[0], vertical_v),
                (inject.at[0], inject_v),
                (diffuse, mix_n),
                (substeps, sub_n),
                (landmask, wet_v),
                (forcing, force_n),
                (extract.at[0], extract_v),
                (weights, weights_v),
                (links, links_s),
            )
        )
    ]
    def load(g):
        return pltpu.make_async_copy(state.at[g], natural.at[g], load_sem.at[g])

    for copy in small[:6]:
        copy.start()
    for g in range(groups):
        load(g).start()
    for copy in small[6:]:
        copy.start()

    barrier = pltpu.get_barrier_semaphore()
    for side in (left, right):
        pl.semaphore_signal(barrier, inc=1, device_id=(comp, side), device_id_type=MESH)

    def greet(p, carry):
        peer = first + p
        pl.semaphore_signal(
            barrier, inc=1, device_id=(peer // doms, peer % doms), device_id_type=MESH
        )
        return carry

    lax.fori_loop(0, count, greet, 0)

    blank_tile = jnp.zeros((groups, 8, LANES), F32)
    for field in (end_0, end_1):
        field[:, 0] = blank_tile
        field[:, ENDS - 1] = blank_tile
    for copy in small[:6]:
        copy.wait()
    mix_v[...] = jnp.transpose(mix_n[...])
    sub_v[...] = jnp.transpose(sub_n[...].astype(F32))
    for t in range(tiles):
        force_n[t] = force_n[t] * wet_v[t].astype(F32)
    for u in range(8):
        flip(force_v, u, force_n, u, tiles)
    eye = (
        lax.broadcasted_iota(jnp.int32, (levels, levels), 0)
        == lax.broadcasted_iota(jnp.int32, (levels, levels), 1)
    ).astype(F32)
    left_b = stack_left(
        left_f,
        (
            (0, vertical_v[...] * DT + eye),
            (levels, jnp.transpose(inject_v[...])[0:levels] * DT),
        ),
    )
    sides = [
        pltpu.make_async_remote_copy(
            src_ref=edge.at[k],
            dst_ref=halo.at[k],
            send_sem=halo_send.at[k],
            recv_sem=halo_recv.at[k],
            device_id=(comp, side),
            device_id_type=MESH,
        )
        for k, side in enumerate((right, left))
    ]

    def send_sides():
        for k, at in enumerate((tiles - 1, 0)):
            row = slice(at, at + 1)
            edge[k, 0:levels] = natural[:, at].reshape(levels, LANES)
            edge[k, levels : levels + 8] = force_n[at]
            edge[k, levels + 8 : levels + 16] = jnp.broadcast_to(mix_n[row], (8, LANES))
            edge[k, levels + 16 : levels + 24] = jnp.broadcast_to(
                sub_n[row].astype(F32), (8, LANES)
            )
        for copy in sides:
            copy.start()

    def take_sides():
        for copy in sides:
            copy.wait()
        for at, part in ((1, halo.at[0]), (2, edge.at[1]), (3, edge.at[0]), (4, halo.at[1])):
            there = slice(at * LANES, (at + 1) * LANES)
            end_0[:, at] = part[0:levels].reshape(levels // 8, 8, LANES)
            end_force[:, there] = part[levels : levels + 8]
            end_mix[:, there] = part[levels + 8 : levels + 9]
            end_sub[:, there] = part[levels + 16 : levels + 17].astype(jnp.int32)

    def split(s, carry):
        high, low = high_low(weights_v[s])
        split_w[s, 0:LANES] = high
        split_w[s, LANES:WIDE] = low
        return carry

    def send(p):
        peer = first + p
        return pltpu.make_async_remote_copy(
            src_ref=msg.at[p],
            dst_ref=arrived.at[me],
            send_sem=msg_send.at[p],
            recv_sem=msg_recv.at[me],
            device_id=(peer // doms, peer % doms),
            device_id_type=MESH,
        )

    lane = lax.broadcasted_iota(jnp.int32, (8, LANES), 1)
    blank = jnp.zeros((PAD_ROWS - levels, LANES), F32)

    def form(step, pick_b):
        rows = []
        for q in range(GROUP):
            peer = first + step * GROUP + q
            for k in range(2):
                block = jnp.maximum(links_s[0, 0, k, peer], 0)
                x = natural[:, block].reshape(levels, LANES)
                wet = wet_v[block]
                high, low = high_low(jnp.concatenate([x, blank], axis=0))
                rows.append((jnp.concatenate([high, low, high], axis=0), wet))
        outs = []
        for m in range(0, 2 * GROUP, 2):
            both = jnp.dot(
                pick_b,
                jnp.concatenate([rows[m][0], rows[m + 1][0]], axis=1),
                preferred_element_type=F32,
            )
            for k in range(2):
                r = both[:, k * LANES : (k + 1) * LANES] * rows[m + k][1].astype(F32)
                high = r.astype(BF16).astype(F32)
                low = r - high
                top = jnp.concatenate([high, high], axis=1)
                bottom = jnp.concatenate([low, jnp.zeros_like(low)], axis=1)
                lhs = jnp.concatenate([top, bottom], axis=0).astype(BF16)
                slot = jnp.maximum(links_s[2, 0, k, first + step * GROUP + m // 2], 0)
                out = jnp.dot(lhs, split_w[slot], preferred_element_type=F32)
                outs.append(out[0:8] + out[8:16])
        for q in range(GROUP):
            p = step * GROUP + q
            peer = first + p
            t0 = jnp.where(lane == 0, links_s[1, 0, 0, peer].astype(F32), -1.0)
            t1 = jnp.where(lane == 1, links_s[1, 0, 1, peer].astype(F32), t0)
            msg[p] = jnp.concatenate(outs[2 * q : 2 * q + 2] + [t1], axis=0)

    def start(step):
        for q in range(GROUP):
            send(step * GROUP + q).start()

    def form_next(step, pick_b):
        start(step - 1)
        form(step, pick_b)
        return pick_b

    def send_all():
        for copy in small[6:]:
            copy.wait()
        pick_b = stack_left(pick_f, ((0, extract_v[...]),))
        lax.fori_loop(0, weights_v.shape[0], split, 0, unroll=4)
        form(0, pick_b)
        pl.semaphore_wait(barrier, count + 2)
        send_sides()
        lax.fori_loop(1, count // GROUP, form_next, pick_b)
        start(count // GROUP - 1)

    def enter(step, carry):
        for v in range(BATCH):
            load(step * BATCH + v).wait()
        for v in range(BATCH):
            g = step * BATCH + v
            for u in range(8):
                flip(field_0, (g * (tiles + 2) + 1) * 8 + u, natural, g * tiles * 8 + u, tiles)
        return carry

    lax.fori_loop(0, groups // BATCH, enter, 0)

    def run(src, dst, j, early):
        last = src[:, tiles].reshape(levels, LANES)
        src[:, 0] = pltpu.roll(last, 1, axis=1).reshape(groups, 8, LANES)
        following = src[:, 1].reshape(levels, LANES)
        src[:, tiles + 1] = pltpu.roll(following, LANES - 1, axis=1).reshape(groups, 8, LANES)
        stage = j.astype(F32)

        def part(i, carry):
            at = i * STEP
            if early:

                @pl.when((j == 0) & (i == 0))
                def _():
                    send_all()

            substep(
                src,
                dst,
                1 + at,
                STEP,
                lambda t: force_v[at + t],
                lambda t: mix_v[pl.ds(at + t, 1), :],
                lambda t: sub_v[pl.ds(at + t, 1), :] > stage,
                left_b,
            )
            return carry

        lax.fori_loop(0, runs, part, 0)

    def twice(pair, carry):
        run(field_0, field_1, 2 * pair, True)

        run(field_1, field_0, 2 * pair + 1, False)
        return carry

    lax.fori_loop(0, SUBS // 2, twice, 0)
    take_sides()

    def end_twice(pair, carry):
        end_substep(end_0, end_1, end_force, end_mix, end_sub, 2 * pair, left_b)
        end_substep(end_1, end_0, end_force, end_mix, end_sub, 2 * pair + 1, left_b)
        return carry

    lax.fori_loop(0, SUBS // 2, end_twice, 0)
    end_out[:, 0] = end_0[:, 2]
    end_out[:, 1] = end_0[:, 3]

    def finish(p, carry):
        send(p).wait_send()
        g = first + p
        pltpu.make_async_copy(arrived.at[g], arrived.at[g], msg_recv.at[g]).wait()
        return carry

    lax.fori_loop(0, count, finish, 0)
    fields = inject.shape[1]
    targets[...] = arrived[:, 2 * fields, :].astype(jnp.int32)


def interval(comps, doms, links, state, forcing, vertical, inject, extract, diffuse, substeps, landmask, weights):
    groups, tiles = state.shape[:2]
    levels, fields = vertical.shape[1], forcing.shape[1]
    slots = weights.shape[0]
    devices = comps * doms
    peers = max(doms, devices - doms)
    stack = (groups, tiles + 2, 8, LANES)
    ends = (groups, ENDS, 8, LANES)
    square = (tiles, LANES)
    hbm = pl.BlockSpec(memory_space=pltpu.HBM)
    vmem = pl.BlockSpec(memory_space=pltpu.VMEM)
    edge_rows = levels + 24
    return pl.pallas_call(
        functools.partial(interval_kernel, comps, doms),
        out_shape=(
            pltpu.VMEM(stack, F32),
            pltpu.VMEM((devices, 2 * fields + 8, LANES), F32),
            pltpu.VMEM((devices, LANES), jnp.int32),
            pltpu.VMEM((groups, 2, 8, LANES), F32),
        ),
        in_specs=[hbm] * 10,
        out_specs=(vmem, vmem, vmem, vmem),
        scratch_shapes=[
            pltpu.VMEM(state.shape, F32),
            pltpu.VMEM(stack, F32),
            pltpu.VMEM(ends, F32),
            pltpu.VMEM(ends, F32),
            pltpu.VMEM((fields, ENDS * LANES), F32),
            pltpu.VMEM((1, ENDS * LANES), F32),
            pltpu.VMEM((1, ENDS * LANES), jnp.int32),
            pltpu.SMEM(links.shape, jnp.int32),
            pltpu.VMEM(forcing.shape, F32),
            pltpu.VMEM(forcing.shape, F32),
            pltpu.VMEM(square, F32),
            pltpu.VMEM(square, F32),
            pltpu.VMEM(square, jnp.int32),
            pltpu.VMEM(square, F32),
            pltpu.VMEM((tiles, 1, LANES), jnp.int32),
            pltpu.VMEM((levels, levels), F32),
            pltpu.VMEM((fields, levels), F32),
            pltpu.VMEM((fields, levels), F32),
            pltpu.VMEM(weights.shape, F32),
            pltpu.VMEM((slots, WIDE, LANES), BF16),
            pltpu.VMEM((levels, WIDE), F32),
            pltpu.VMEM((fields, WIDE), F32),
            pltpu.VMEM((peers, 2 * fields + 8, LANES), F32),
            pltpu.VMEM((2, edge_rows, LANES), F32),
            pltpu.VMEM((2, edge_rows, LANES), F32),
            pltpu.SemaphoreType.DMA((groups,)),
            pltpu.SemaphoreType.DMA((9,)),
            pltpu.SemaphoreType.DMA((peers,)),
            pltpu.SemaphoreType.DMA((devices,)),
            pltpu.SemaphoreType.DMA((2,)),
            pltpu.SemaphoreType.DMA((2,)),
        ],
        compiler_params=pltpu.CompilerParams(
            collective_id=0, has_side_effects=True, vmem_limit_bytes=40 << 20
        ),
        name="interval",
    )(
        *(
            pltpu.with_memory_space_constraint(a, pltpu.HBM)
            for a in (
                links, state, forcing, vertical, inject, extract, diffuse, substeps, landmask, weights
            )
        )
    )


def deliver_kernel(
    comps, doms, targets, arrived, result, ends, state_next, forcing_next, targets_s, next_v, natural, sems
):
    groups, tiles = state_next.shape[:2]
    get_targets = pltpu.make_async_copy(targets, targets_s, sems.at[0])
    get_targets.start()

    def store(g):
        return pltpu.make_async_copy(natural.at[g], state_next.at[g], sems.at[3 + g])

    near = lax.broadcasted_iota(jnp.int32, (8, LANES), 1) < LANES // 2

    def leave(step, carry):
        for v in range(BATCH):
            g = step * BATCH + v
            for u in range(8):
                flip(natural, g * tiles * 8 + u, result, (g * (tiles + 2) + 1) * 8 + u, tiles)
        for v in range(BATCH):
            g = step * BATCH + v
            natural[g, 0] = jnp.where(near, ends[g, 0], natural[g, 0])
            natural[g, tiles - 1] = jnp.where(near, natural[g, tiles - 1], ends[g, 1])
            store(g).start()
        return carry

    lax.fori_loop(0, groups // BATCH, leave, 0)
    next_v[...] = jnp.zeros_like(next_v)
    air = (comps - 1) * doms
    is_air = lax.axis_index("comp") < comps - 1
    count = jnp.where(is_air, doms, air)
    first = jnp.where(is_air, air, 0)
    get_targets.wait()

    def scatter(p, carry):
        for k in range(2):
            t = targets_s[first + p, k]
            there = pl.ds(pl.multiple_of(jnp.maximum(t, 0) * LANES, LANES), LANES)
            part = arrived[first + p, k * 8 : (k + 1) * 8]
            next_v[:, there] += jnp.where(t >= 0, part, jnp.zeros_like(part))
        return carry

    lax.fori_loop(0, count, scatter, 0)
    store_next = pltpu.make_async_copy(next_v, forcing_next, sems.at[2])
    store_next.start()
    for g in range(groups):
        store(g).wait()
    store_next.wait()


def deliver(comps, doms, targets, arrived, result, ends, fields):
    hbm = pl.BlockSpec(memory_space=pltpu.HBM)
    vmem = pl.BlockSpec(memory_space=pltpu.VMEM)
    groups, tiles = result.shape[0], result.shape[1] - 2
    columns = tiles * LANES
    return pl.pallas_call(
        functools.partial(deliver_kernel, comps, doms),
        out_shape=(
            jax.ShapeDtypeStruct((groups, tiles, 8, LANES), F32),
            jax.ShapeDtypeStruct((fields, columns), F32),
        ),
        in_specs=[vmem] * 4,
        out_specs=(hbm, hbm),
        scratch_shapes=[
            pltpu.SMEM(targets.shape, jnp.int32),
            pltpu.VMEM((fields, columns), F32),
            pltpu.VMEM((groups, tiles, 8, LANES), F32),
            pltpu.SemaphoreType.DMA((3 + groups,)),
        ],
        compiler_params=pltpu.CompilerParams(vmem_limit_bytes=12 << 20),
        name="deliver",
    )(
        *(
            pltpu.with_memory_space_constraint(a, pltpu.VMEM)
            for a in (targets, arrived, result, ends)
        )
    )


def solution(mesh):
    comps, doms = mesh.shape["comp"], mesh.shape["dom"]

    def local(state, forcing, vertical, inject, extract, diffuse, substeps, landmask, links, weights):
        levels, columns = state.shape
        tiles = state.reshape(levels // 8, 8, columns // LANES, LANES).swapaxes(1, 2)
        result, arrived, targets, ends = interval(
            comps,
            doms,
            links.swapaxes(2, 3),
            tiles,
            forcing.reshape(-1, columns // LANES, LANES).swapaxes(0, 1),
            vertical,
            inject.swapaxes(1, 2),
            extract,
            diffuse.reshape(-1, LANES),
            substeps.reshape(-1, LANES),
            landmask.reshape(-1, 1, LANES),
            weights,
        )
        new, forcing_next = deliver(comps, doms, targets, arrived, result, ends, forcing.shape[0])
        return new.swapaxes(1, 2).reshape(state.shape), forcing_next

    return jax.shard_map(
        local,
        mesh=mesh,
        in_specs=(
            P(None, ("comp", "dom")),
            P(None, ("comp", "dom")),
            P("comp", None, None),
            P("comp", None, None),
            P("comp", None, None),
            P(("comp", "dom")),
            P(("comp", "dom")),
            P(("comp", "dom")),
            P(None, ("comp", "dom"), None, None),
            P(("comp", "dom"), None, None),
        ),
        out_specs=(P(None, ("comp", "dom")), P(None, ("comp", "dom"))),
        check_vma=False,
    )
```
